768 devices in a mesh: ta: 16 (over y, core), ha: 48 (over x, z).
Axes of the slice: x: 4, y: 8, z: 12, core: 2. Of those that a mesh axis runs over, the one named last changes fastest.
Arguments:
- query_states: bfloat16 [32, 96, 56, 768], P('ta', 'ha'), may hold values from -51 to 51
- key_states: bfloat16 [32, 96, 56, 768], P('ta', 'ha'), may hold values from -6 to 6
- value_states: bfloat16 [32, 96, 56, 768], P('ta', 'ha'), may hold values from -6 to 6
- conv_weight: bfloat16 [27, 768], replicated, may hold values from -1.1953125 to 1.1953125
- out_grad: bfloat16 [32, 96, 56, 768], P('ta', 'ha'), may hold values from -6 to 6
- tile_mask: int32 [16, 48, 9], replicated, may hold values from 0 to 1, as said below
- clip_lengths: int32 [32], replicated, may hold values from 2 to 56
Outputs:
- layer_out: bfloat16 [32, 96, 56, 768], P('ta', 'ha')
- query_grad: bfloat16 [32, 96, 56, 768], P('ta', 'ha')
- key_grad: bfloat16 [32, 96, 56, 768], P('ta', 'ha')
- value_grad: bfloat16 [32, 96, 56, 768], P('ta', 'ha')
The draws below stay inside these ranges and needn't reach their ends.
Inputs may be any that keep to these rules, and one draw needn't show every extreme that they name: `tile_mask`: entries are 0 or 1; entry 4, a tile's own keys, is always 1.
All inputs are finite; a program needn't handle non-finite values.
Results may differ from the reference program's by a relative error of at most 0.0095.
Values may be sent and summed in bfloat16 or wider, within the bound.
A program may use at most 128 MiB of HBM per device.

```python
import jax
import jax.numpy as jnp
from jax import lax

HEAD_COUNT = 6
HEAD_DIM = 128
CHANNELS = 768
TILE_SIDE = 2
WIDTH_CELLS = 56
TIME_TILES = 16
HEIGHT_TILES = 48
FRAMES = 32
LATENT_ROWS = 96
N_TA = 16
N_HA = 48


def shared_states(key):
    shape = (FRAMES, LATENT_ROWS, WIDTH_CELLS, CHANNELS)
    key_query = jax.random.fold_in(key, 11)
    key_keys = jax.random.fold_in(key, 12)
    query_f = jnp.clip(jax.random.normal(key_query, shape, jnp.float32), -6.0, 6.0)
    keys_f = jnp.clip(jax.random.normal(key_keys, shape, jnp.float32), -6.0, 6.0)
    return (query_f, keys_f)


def draw_query_states(key, part):
    return shared_states(key)[0].astype(jnp.bfloat16)


def draw_key_states(key, part):
    return shared_states(key)[1].astype(jnp.bfloat16)


def draw_tile_mask(key, part):
    level = jax.random.randint(jax.random.fold_in(key, 21), (TIME_TILES, HEIGHT_TILES, 1), 0, 3)
    picked = jax.random.randint(jax.random.fold_in(key, 22), (TIME_TILES, HEIGHT_TILES, 9), 0, 9)
    kept_tiles = (picked < 2 + 3 * level).astype(jnp.int32)
    centre = jnp.arange(9) == 4
    return jnp.where(centre[None, None, :], 1, kept_tiles).astype(jnp.int32)


def draw_clip_lengths(key, part):
    lengths = jax.random.randint(jax.random.fold_in(key, 31), (FRAMES,), 2, WIDTH_CELLS + 1)
    order = jax.random.permutation(jax.random.fold_in(key, 32), FRAMES)
    lengths = lengths.at[order[0]].set(WIDTH_CELLS)
    lengths = lengths.at[order[1]].set(2)
    return lengths.astype(jnp.int32)


def steps_of(own_key, extent, shards, smallest, high):
    def one(position, parts):
        steps = jax.random.uniform(jax.random.fold_in(jax.random.fold_in(own_key, 6), position), (parts,), jnp.float32, smallest / len(shards), high / len(shards))
        return jnp.repeat(jnp.exp(steps), extent[position] // parts).reshape((-1,) + (1,) * (len(extent) - position - 1))

    factor_of = one(*shards[0])
    for cut in shards[1:]:
        factor_of = factor_of * one(*cut)
    return factor_of


def centred(key, extent, deviation, limit, shards=(), kind=jnp.bfloat16):
    values = deviation * jax.random.normal(key, extent, jnp.float32)
    if shards:
        values = values * steps_of(key, extent, shards, -0.22, 0.18)
    return jnp.clip(values, -limit, limit).astype(kind)


def setup_inputs(seed: int = 0) -> dict:
    seeds = jax.random.split(jax.random.key(seed), 8)
    query_states = draw_query_states(jax.random.fold_in(seeds[7], 71), 0)
    key_states = draw_key_states(jax.random.fold_in(seeds[7], 71), 0)
    value_states = centred(seeds[2], (FRAMES, LATENT_ROWS, WIDTH_CELLS, CHANNELS), 1.0, 6.0, ((0, 16), (1, 48)))
    conv_weight = centred(seeds[3], (27, CHANNELS), 0.2, 1.1953125)
    out_grad = centred(seeds[4], (FRAMES, LATENT_ROWS, WIDTH_CELLS, CHANNELS), 1.0, 6.0, ((0, 16), (1, 48)))
    tile_mask = draw_tile_mask(jax.random.fold_in(seeds[7], 71), 0)
    clip_lengths = draw_clip_lengths(jax.random.fold_in(seeds[7], 71), 0)
    return dict(query_states=query_states, key_states=key_states, value_states=value_states, conv_weight=conv_weight, out_grad=out_grad, tile_mask=tile_mask, clip_lengths=clip_lengths)


def starts(*values):
    return tuple(jnp.asarray(value).astype(jnp.int32) for value in values)


def depthwise(source, weight, size_t, size_h, width_len):
    result = jnp.zeros((size_t, size_h, width_len, source.shape[3]), jnp.float32)
    for offset_id in range(27):
        step_t, step_h, step_w = offset_id // 9, (offset_id // 3) % 3, offset_id % 3
        piece = source[step_t:step_t + size_t, step_h:step_h + size_h, step_w:step_w + width_len].astype(jnp.float32)
        result = result + weight[offset_id].astype(jnp.float32) * piece
    return result


def source_conv(grad_window, weight, tile_side, width_len):
    slab = grad_window[tile_side - 1:2 * tile_side + 1, tile_side - 1:2 * tile_side + 1].astype(jnp.float32)
    slab = jnp.pad(slab, ((0, 0), (0, 0), (1, 1), (0, 0)))
    result = jnp.zeros((3, 3, tile_side, tile_side, width_len, slab.shape[3]), jnp.float32)
    three = jnp.arange(3)
    for offset_id in range(27):
        step_t, step_h, step_w = offset_id // 9, (offset_id // 3) % 3, offset_id % 3
        piece = slab[step_t:step_t + tile_side, step_h:step_h + tile_side, step_w:step_w + width_len]
        piece = weight[26 - offset_id].astype(jnp.float32) * piece
        tiles_t = (tile_side - 1 + step_t + jnp.arange(tile_side)) // tile_side
        tiles_h = (tile_side - 1 + step_h + jnp.arange(tile_side)) // tile_side
        pick_t = (tiles_t[None, :] == three[:, None]).astype(jnp.float32)
        pick_h = (tiles_h[None, :] == three[:, None]).astype(jnp.float32)
        result = result + pick_t[:, None, :, None, None, None] * pick_h[None, :, None, :, None, None] * piece[None, None]
    return result


def combine_tiles(terms):
    three = jnp.arange(3)
    centre = (three[:, None] == 1) & (three[None, :] == 1)
    rounded = lax.optimization_barrier(terms.astype(jnp.bfloat16)).astype(jnp.float32)
    return jnp.sum(jnp.where(centre[:, :, None, None, None, None], terms, rounded), axis=(0, 1))


def to_grid(stacked):
    last_dim = stacked.shape[-1]
    shaped = stacked.reshape(N_TA, N_HA, TILE_SIDE, TILE_SIDE, WIDTH_CELLS, last_dim)
    return shaped.transpose(0, 2, 1, 3, 4, 5).reshape(TILE_SIDE * N_TA, TILE_SIDE * N_HA, WIDTH_CELLS, last_dim)


def reference(query_states, key_states, value_states, conv_weight, out_grad, tile_mask, clip_lengths):
    score_scale = HEAD_DIM ** -0.5
    window_len = 3 * TILE_SIDE
    channels = HEAD_COUNT * HEAD_DIM
    queries = TILE_SIDE * TILE_SIDE * WIDTH_CELLS
    pad_grid = ((TILE_SIDE, TILE_SIDE), (TILE_SIDE, TILE_SIDE), (0, 0), (0, 0))
    query_pad = jnp.pad(query_states, pad_grid)
    key_pad = jnp.pad(key_states, pad_grid)
    value_pad = jnp.pad(value_states, pad_grid)
    grad_pad = jnp.pad(out_grad, pad_grid)
    lens_pad = jnp.pad(clip_lengths, (TILE_SIDE, TILE_SIDE))
    mask_pad = jnp.pad(tile_mask, ((1, 1), (1, 1), (0, 0)))
    tile_offset = jnp.arange(window_len) // TILE_SIDE
    columns = jnp.arange(WIDTH_CELLS)

    def query_pass(tile_id):
        tile_t = tile_id // N_HA
        tile_h = tile_id % N_HA
        own_start = starts(tile_t * TILE_SIDE + TILE_SIDE, tile_h * TILE_SIDE + TILE_SIDE, 0, 0)
        win_start = starts(tile_t * TILE_SIDE, tile_h * TILE_SIDE, 0, 0)
        own_size = (TILE_SIDE, TILE_SIDE, WIDTH_CELLS, channels)
        win_size = (window_len, window_len, WIDTH_CELLS, channels)
        query_f = lax.dynamic_slice(query_pad, own_start, own_size).reshape(queries, HEAD_COUNT, HEAD_DIM).astype(jnp.float32)
        grad_f = lax.dynamic_slice(grad_pad, own_start, own_size).reshape(queries, HEAD_COUNT, HEAD_DIM).astype(jnp.float32)
        key_f = lax.dynamic_slice(key_pad, win_start, win_size).reshape(-1, HEAD_COUNT, HEAD_DIM).astype(jnp.float32)
        value_f = lax.dynamic_slice(value_pad, win_start, win_size).reshape(-1, HEAD_COUNT, HEAD_DIM).astype(jnp.float32)
        frame_lens = lax.dynamic_slice(lens_pad, starts(tile_t * TILE_SIDE), (window_len,))
        entries = mask_pad[tile_t + 1, tile_h + 1].reshape(3, 3)
        kept_tiles = entries[tile_offset][:, tile_offset] == 1
        height_ids = tile_h + tile_offset - 1
        in_height = (height_ids >= 0) & (height_ids < N_HA)
        key_valid = kept_tiles[:, :, None] & in_height[None, :, None] & (columns[None, None, :] < frame_lens[:, None, None])
        key_valid = key_valid.reshape(-1)
        scores = jnp.einsum("qhd,khd->hqk", query_f, key_f) * score_scale
        scores = jnp.where(key_valid[None, None, :], scores, -jnp.inf)
        row_max = jnp.max(scores, axis=-1, keepdims=True)
        exponent = jnp.exp(scores - row_max)
        row_total = jnp.sum(exponent, axis=-1, keepdims=True)
        softmax_p = exponent / row_total
        probs_bf = softmax_p.astype(jnp.bfloat16)
        attention = jnp.einsum("hqk,khd->qhd", probs_bf.astype(jnp.float32), value_f)
        row_delta = jnp.sum(grad_f * attention, axis=-1)
        dprobs = jnp.einsum("qhd,khd->hqk", grad_f, value_f)
        dscores = (softmax_p * (dprobs - row_delta.T[:, :, None])).astype(jnp.bfloat16)
        query_part = jnp.einsum("hqk,khd->qhd", dscores.astype(jnp.float32), key_f) * score_scale
        log_total = (row_max[..., 0] + jnp.log(row_total[..., 0])).T
        tile_shape = (TILE_SIDE, TILE_SIDE, WIDTH_CELLS)
        return (attention.reshape(tile_shape + (channels,)), query_part.astype(jnp.bfloat16).reshape(tile_shape + (channels,)),
                log_total.reshape(tile_shape + (HEAD_COUNT,)), row_delta.reshape(tile_shape + (HEAD_COUNT,)))

    tile_ids = jnp.arange(N_TA * N_HA, dtype=jnp.int32)
    attention_t, query_t, total_t, delta_t = lax.map(query_pass, tile_ids)
    attention_grid = to_grid(attention_t)
    query_grad = to_grid(query_t)
    total_pad = jnp.pad(to_grid(total_t), pad_grid)
    delta_pad = jnp.pad(to_grid(delta_t), pad_grid)

    def key_pass(tile_id):
        tile_t = tile_id // N_HA
        tile_h = tile_id % N_HA
        own_start = starts(tile_t * TILE_SIDE + TILE_SIDE, tile_h * TILE_SIDE + TILE_SIDE, 0, 0)
        win_start = starts(tile_t * TILE_SIDE, tile_h * TILE_SIDE, 0, 0)
        own_size = (TILE_SIDE, TILE_SIDE, WIDTH_CELLS, channels)
        win_size = (window_len, window_len, WIDTH_CELLS, channels)
        stat_size = (window_len, window_len, WIDTH_CELLS, HEAD_COUNT)
        key_f = lax.dynamic_slice(key_pad, own_start, own_size).reshape(queries, HEAD_COUNT, HEAD_DIM).astype(jnp.float32)
        value_f = lax.dynamic_slice(value_pad, own_start, own_size).reshape(queries, HEAD_COUNT, HEAD_DIM).astype(jnp.float32)
        near_query = lax.dynamic_slice(query_pad, win_start, win_size).reshape(-1, HEAD_COUNT, HEAD_DIM).astype(jnp.float32)
        grad_window = lax.dynamic_slice(grad_pad, win_start, win_size)
        near_grad = grad_window.reshape(-1, HEAD_COUNT, HEAD_DIM).astype(jnp.float32)
        near_total = lax.dynamic_slice(total_pad, win_start, stat_size).reshape(-1, HEAD_COUNT).T
        near_delta = lax.dynamic_slice(delta_pad, win_start, stat_size).reshape(-1, HEAD_COUNT).T
        nearby = lax.dynamic_slice(mask_pad, starts(tile_t, tile_h, 0), (3, 3, 9)).reshape(9, 9)
        facing = nearby[jnp.arange(9), 8 - jnp.arange(9)].reshape(3, 3)
        query_ok = jnp.broadcast_to((facing[tile_offset][:, tile_offset] == 1)[:, :, None], (window_len, window_len, WIDTH_CELLS)).reshape(-1)
        frame_lens = lax.dynamic_slice(lens_pad, starts(tile_t * TILE_SIDE + TILE_SIDE), (TILE_SIDE,))
        key_ok = jnp.broadcast_to(columns[None, None, :] < frame_lens[:, None, None], (TILE_SIDE, TILE_SIDE, WIDTH_CELLS)).reshape(-1)
        visible = query_ok[:, None] & key_ok[None, :]
        scores = jnp.einsum("qhd,khd->hqk", near_query, key_f) * score_scale
        softmax_p = jnp.exp(jnp.where(visible[None], scores - near_total[:, :, None], -jnp.inf))
        probs_bf = softmax_p.astype(jnp.bfloat16)
        dprobs = jnp.einsum("qhd,khd->hqk", near_grad, value_f)
        dscores = (softmax_p * (dprobs - near_delta[:, :, None])).astype(jnp.bfloat16)
        split_q = (HEAD_COUNT, 3, TILE_SIDE, 3, TILE_SIDE, WIDTH_CELLS, queries)
        split_rows = (3, TILE_SIDE, 3, TILE_SIDE, WIDTH_CELLS, HEAD_COUNT, HEAD_DIM)
        tiles_shape = (3, 3, TILE_SIDE, TILE_SIDE, WIDTH_CELLS, channels)
        key_tiles = jnp.einsum("haibjwk,aibjwhd->abkhd", dscores.astype(jnp.float32).reshape(split_q),
                               near_query.reshape(split_rows)) * score_scale
        value_tiles = jnp.einsum("haibjwk,aibjwhd->abkhd", probs_bf.astype(jnp.float32).reshape(split_q),
                                 near_grad.reshape(split_rows))
        value_tiles = value_tiles.reshape(tiles_shape) + source_conv(grad_window, conv_weight, TILE_SIDE, WIDTH_CELLS)
        return combine_tiles(key_tiles.reshape(tiles_shape)), combine_tiles(value_tiles)

    key_t, value_t = lax.map(key_pass, tile_ids)
    key_grad = to_grid(key_t).astype(jnp.bfloat16)
    one_pad = ((1, 1), (1, 1), (1, 1), (0, 0))
    frames = TILE_SIDE * N_TA
    rows = TILE_SIDE * N_HA
    conv_out = depthwise(jnp.pad(value_states, one_pad), conv_weight, frames, rows, WIDTH_CELLS)
    layer_out = (attention_grid + conv_out).astype(jnp.bfloat16)
    value_grad = to_grid(value_t).astype(jnp.bfloat16)
    return layer_out, query_grad, key_grad, value_grad
```

```python
import functools
import math

import jax
import jax.numpy as jnp
from jax import lax
from jax.experimental import pallas as pl
from jax.experimental.pallas import tpu as pltpu
from jax.sharding import PartitionSpec as P

MESH = pl.DeviceIdType.MESH
HEAD_DIM = 128
TILE_SIDE = 2
F32 = jnp.float32
BF16 = jnp.bfloat16
BIG = 1e30
LOG2E = math.log2(math.e)

AK, AV, AQ, AG = 0, 1, 2, 3
OWN, L, R, PP, PL_, PR, OO, OL, OR = range(9)

LAST = (((1,), (1,)), ((), ()))


def nt(a, b):
    return lax.dot_general(a, b, LAST, preferred_element_type=F32)


def nn(a, b):
    return jnp.dot(a, b, preferred_element_type=F32)


def kernel(
    heads, cells, rows, padded, n_t, n_h, chunks,
    q_hbm, k_hbm, v_hbm, w_hbm, g_hbm, mask_hbm, clip_hbm,
    out_hbm, dq_hbm, dk_hbm, dv_hbm,
    tiles, probs, dprobs, slot_max, top, total, attn, delta, key_acc, value_acc, staged,
    bias, penalty, stat_mat, stat_out, stat_in, w_ref, wf_ref, mask_ref, clip_ref,
    load_sem, aux_sem, store_sem, send_sem, recv_sem, stat_send, stat_recv,
):
    scale = HEAD_DIM ** -0.5
    c2 = scale * LOG2E
    t = lax.axis_index("ta")
    h = lax.axis_index("ha")
    parity = lax.rem(t, 2)
    a_p = 1 - 2 * parity
    a_rows = (0, a_p, -a_p)
    b_cols = (0, -1, 1)
    t_rows = tuple(lax.rem(t + a + n_t, n_t) for a in a_rows)
    h_cols = tuple(lax.rem(h + b + n_h, n_h) for b in b_cols)
    flip = (0, 2, 1)
    hpc = heads // chunks

    def load(arr, hd):
        src = (k_hbm, v_hbm, q_hbm, g_hbm)[arr]
        return pltpu.make_async_copy(
            src.at[:, pl.ds(hd * HEAD_DIM, HEAD_DIM)],
            tiles.at[arr, OWN, hd, pl.ds(0, rows)],
            load_sem.at[arr, hd],
        )

    for arr in (AK, AV, AQ, AG):
        for hd in range(heads):
            load(arr, hd).start()
    aux = (
        pltpu.make_async_copy(mask_hbm, mask_ref, aux_sem.at[0]),
        pltpu.make_async_copy(clip_hbm, clip_ref, aux_sem.at[1]),
        pltpu.make_async_copy(w_hbm, w_ref, aux_sem.at[2]),
    )
    for copy in aux:
        copy.start()

    barrier = pltpu.get_barrier_semaphore()
    for slot in range(1, 9):
        pl.semaphore_signal(
            barrier, inc=1, device_id=(t_rows[slot // 3], h_cols[slot % 3]), device_id_type=MESH
        )
    pl.semaphore_wait(barrier, 8)

    def travel(arr, src_slot, to, chunk):
        row, col = src_slot // 3, src_slot % 3
        if to in (L, R):
            dst_slot = 3 * row + flip[to]
            device = (t, h_cols[to])
        else:
            dst_slot = to + col
            device = (t_rows[to // 3], h)
        part = (pl.ds(chunk * hpc, hpc), pl.ds(0, rows))
        return pltpu.make_async_remote_copy(
            src_ref=tiles.at[(arr, src_slot) + part],
            dst_ref=tiles.at[(arr, dst_slot) + part],
            send_sem=send_sem.at[arr, dst_slot, chunk],
            recv_sem=recv_sem.at[arr, dst_slot, chunk],
            device_id=device,
            device_id_type=MESH,
        )

    sent = []

    def send(arr, src_slot, targets):
        for chunk in range(chunks):
            send_chunk(arr, src_slot, targets, chunk)

    def send_chunk(arr, src_slot, targets, chunk):
        for to in targets:
            copy = travel(arr, src_slot, to, chunk)
            copy.start()
            sent.append(copy)

    def arrived_chunk(arr, slot, chunk):
        part = (pl.ds(chunk * hpc, hpc), pl.ds(0, rows))
        place = tiles.at[(arr, slot) + part]
        pltpu.make_async_remote_copy(
            src_ref=place, dst_ref=place,
            send_sem=send_sem.at[arr, slot, chunk], recv_sem=recv_sem.at[arr, slot, chunk],
            device_id=(t, h_cols[1]), device_id_type=MESH,
        ).wait_recv()

    def arrived(arr, slot):
        for chunk in range(chunks):
            arrived_chunk(arr, slot, chunk)

    for arr, targets in ((AK, (OO, L, R, PP)), (AV, (OO, L, R, PP)), (AQ, (L, R, PP)), (AG, (L, R, PP))):
        for hd in range(heads):
            load(arr, hd).wait()
        send(arr, OWN, targets)

    @pl.loop(0, 4 * 9)
    def _(i):
        tiles[i // 9, i % 9, :, pl.ds(rows, padded - rows), :] = jnp.zeros(
            (heads, padded - rows, HEAD_DIM), BF16
        )

    @pl.loop(0, heads)
    def _(hd):
        zero = jnp.zeros((rows, HEAD_DIM), F32)
        top[hd] = zero - BIG
        total[hd] = zero
        attn[hd] = zero
        key_acc[hd] = zero
        value_acc[hd] = zero

    for copy in aux:
        copy.wait()

    lane = lax.broadcasted_iota(jnp.int32, (1, padded), 1)
    tile_frame = (lane >= 2 * cells).astype(jnp.int32)
    column = lane - cells * (
        (lane >= cells).astype(jnp.int32) + tile_frame + (lane >= 3 * cells).astype(jnp.int32)
    )
    shape = mask_ref.shape[1:]
    it = lax.broadcasted_iota(jnp.int32, shape, 0)
    ih = lax.broadcasted_iota(jnp.int32, shape, 1)

    def frame_len(frame):
        live = clip_ref[jnp.clip(frame, 0, TILE_SIDE * n_t - 1)]
        return jnp.where((frame >= 0) & (frame < TILE_SIDE * n_t), live, 0)

    def entry(index, at_t, at_h):
        here = (it == at_t) & (ih == at_h)
        picked = jnp.where(here, mask_ref[index], 0).astype(F32)
        return jnp.sum(picked, axis=(0, 1), keepdims=True)

    for slot in range(9):
        a, b = a_rows[slot // 3], b_cols[slot % 3]
        index = 3 * (a + 1) + (b + 1)
        first = TILE_SIDE * (t + a)
        len_0, len_1 = frame_len(first), frame_len(first + 1)
        inside = ((h + b >= 0) & (h + b < n_h)).astype(jnp.int32)
        live = jnp.where(tile_frame == 1, len_1 * inside, len_0 * inside)
        seen = (column < live) & (lane < rows)
        keep = jnp.where(seen, entry(index, t, h), 0.0)
        bias[slot] = jnp.where(keep > 0.5, 0.0, -BIG)
        facing = entry(8 - index, t + a, h + b)
        penalty[slot] = jnp.where((lane < rows), jnp.where(facing > 0.5, 0.0, BIG), BIG)

    def forward_slot(slot):
        @pl.loop(0, heads)
        def _(hd):
            q = tiles[AQ, OWN, hd, pl.ds(0, rows), :]
            g = tiles[AG, OWN, hd, pl.ds(0, rows), :]
            k = tiles[AK, slot, hd]
            v = tiles[AV, slot, hd]
            s = nt(q, k) + bias[slot]
            m = jnp.max(s, axis=-1, keepdims=True)
            p = jnp.exp2((s - m) * c2)
            row_sum = jnp.sum(p, axis=-1, keepdims=True)
            p_bf = p.astype(BF16)
            probs[slot, hd] = p_bf
            part = nn(p_bf, v)
            dprobs[slot, hd] = nt(g, v)
            m = jnp.broadcast_to(m, (rows, HEAD_DIM))
            slot_max[slot, hd] = m
            old = top[hd]
            new = jnp.maximum(old, m)
            keep_old = jnp.exp2((old - new) * c2)
            keep_new = jnp.exp2((m - new) * c2)
            top[hd] = new
            total[hd] = total[hd] * keep_old + row_sum * keep_new
            attn[hd] = attn[hd] * keep_old + part * keep_new

    def key_slot(slot):
        @pl.loop(0, heads)
        def _(hd):
            k = tiles[AK, OWN, hd, pl.ds(0, rows), :]
            v = tiles[AV, OWN, hd, pl.ds(0, rows), :]
            q = tiles[AQ, slot, hd]
            g = tiles[AG, slot, hd]
            log_total = stat_in[slot, 2 * hd] + penalty[slot]
            p = jnp.exp2(nt(k, q) * c2 - log_total)
            value_acc[hd] += nn(p.astype(BF16), g)
            ds = p * (nt(v, g) - stat_in[slot, 2 * hd + 1])
            key_acc[hd] += nn(ds.astype(BF16), q)

    def convolve(arr, hd, flipped):
        r_minus, r_plus = 2 - parity, 1 + parity
        in_t = ((t > 0).astype(F32), None, None, (t < n_t - 1).astype(F32))
        in_h = ((h > 0).astype(F32), None, None, (h < n_h - 1).astype(F32))
        source = {}
        for big_i in range(4):
            row = (r_minus, 0, 0, r_plus)[big_i]
            for big_j in range(4):
                col = (1, 0, 0, 2)[big_j]
                i, j = (1, 0, 1, 0)[big_i], (1, 0, 1, 0)[big_j]
                whole = tiles[arr, 3 * row + col, hd, pl.ds(0, rows), :].astype(F32)
                start = (2 * i + j) * cells
                piece = whole[start:start + cells]
                for factor in (in_t[big_i], in_h[big_j]):
                    if factor is not None:
                        piece = piece * factor
                source[big_i, big_j] = piece
        place = lax.broadcasted_iota(jnp.int32, (cells, HEAD_DIM), 0)
        pieces = []
        for i in range(2):
            for j in range(2):
                sums = []
                for dw in range(3):
                    acc = None
                    for dt in range(3):
                        for dh in range(3):
                            o = 9 * dt + 3 * dh + dw
                            o = 26 - o if flipped else o
                            term = source[i + dt, j + dh] * wf_ref[hd, pl.ds(o, 1), :]
                            acc = term if acc is None else acc + term
                    sums.append(acc)
                before = jnp.where(place == 0, 0.0, pltpu.roll(sums[0], 1, 0))
                after = jnp.where(place == cells - 1, 0.0, pltpu.roll(sums[2], cells - 1, 0))
                pieces.append(sums[1] + before + after)
        return pieces

    def store(which, hd):
        dst = (out_hbm, dq_hbm, dk_hbm, dv_hbm)[which]
        return pltpu.make_async_copy(
            staged.at[which, hd],
            dst.at[:, pl.ds(hd * HEAD_DIM, HEAD_DIM)],
            store_sem.at[which, hd],
        )

    def store_all(which):
        for hd in range(heads):
            store(which, hd).start()

    for hd in range(heads):
        wf_ref[hd] = w_ref[:, hd * HEAD_DIM:(hd + 1) * HEAD_DIM].astype(F32)

    forward_slot(OWN)
    arrived(AK, PP)
    arrived(AV, PP)
    forward_slot(PP)
    for chunk in range(chunks):
        for side in (L, R):
            arrived_chunk(AK, side, chunk)
            send_chunk(AK, side, (OO, PP), chunk)
    arrived(AK, OO)
    arrived(AV, OO)
    forward_slot(OO)
    for chunk in range(chunks):
        for side in (L, R):
            arrived_chunk(AV, side, chunk)
            send_chunk(AV, side, (OO, PP), chunk)
    send(AG, OWN, (OO,))
    forward_slot(L)
    forward_slot(R)
    for slot in (PL_, PR, OL, OR):
        arrived(AK, slot)
        arrived(AV, slot)
        forward_slot(slot)

    stat_mat[...] = jnp.zeros_like(stat_mat)

    @pl.loop(0, heads)
    def _(hd):
        g = tiles[AG, OWN, hd, pl.ds(0, rows), :].astype(F32)
        sums = total[hd]
        inverse = 1.0 / sums
        d = jnp.sum(g * attn[hd], axis=-1, keepdims=True) * inverse
        delta[hd] = d
        log_total = top[hd] * c2 + jnp.log(sums) * LOG2E
        lanes = lax.broadcasted_iota(jnp.int32, (rows, HEAD_DIM), 1)
        stat_mat[pl.ds(0, rows), :] = jnp.where(
            lanes == 2 * hd, log_total, jnp.where(lanes == 2 * hd + 1, d, stat_mat[pl.ds(0, rows), :])
        )

    as_rows = stat_mat[...].T
    for i in range(2 * heads):
        stat_out[i] = as_rows[i:i + 1]
        stat_in[OWN, i] = as_rows[i:i + 1]

    def stat_travel(slot):
        row, col = slot // 3, slot % 3
        dst_slot = 3 * row + flip[col]
        return pltpu.make_async_remote_copy(
            src_ref=stat_out,
            dst_ref=stat_in.at[dst_slot],
            send_sem=stat_send.at[dst_slot],
            recv_sem=stat_recv.at[dst_slot],
            device_id=(t_rows[row], h_cols[col]),
            device_id_type=MESH,
        )

    def stat_arrived(slot):
        pltpu.make_async_remote_copy(
            src_ref=stat_in.at[slot], dst_ref=stat_in.at[slot],
            send_sem=stat_send.at[slot], recv_sem=stat_recv.at[slot],
            device_id=(t, h_cols[1]), device_id_type=MESH,
        ).wait_recv()

    for slot in (PP, L, R, OO, PL_, PR, OL, OR):
        stat_travel(slot).start()

    send(AQ, OWN, (OO,))
    for side in (L, R):
        for chunk in range(chunks):
            arrived_chunk(AQ, side, chunk)
            send_chunk(AQ, side, (OO, PP), chunk)
    for chunk in range(chunks):
        arrived_chunk(AG, OO, chunk)
        send_chunk(AG, OO, (L, R), chunk)

    @pl.loop(0, heads)
    def _(hd):
        d = delta[hd]
        d = jnp.concatenate([d, d], axis=1)
        best = top[hd]

        def step(slot, acc):
            ds = probs[slot, hd].astype(F32) * (dprobs[slot, hd] - d)
            part = nn(ds.astype(BF16), tiles[AK, slot, hd])
            return acc + part * jnp.exp2((slot_max[slot, hd] - best) * c2)

        acc = lax.fori_loop(0, 9, step, jnp.zeros((rows, HEAD_DIM), F32))
        staged[1, hd] = (acc * (scale / total[hd])).astype(BF16)

    store_all(1)
    for side in (L, R):
        for chunk in range(chunks):
            arrived_chunk(AG, side, chunk)
            send_chunk(AG, side, (PP,), chunk)

    @pl.loop(0, heads)
    def _(hd):
        pieces = convolve(AV, hd, False)
        whole = jnp.concatenate(pieces, axis=0)
        staged[0, hd] = (attn[hd] / total[hd] + whole).astype(BF16)

    store_all(0)

    key_slot(OWN)
    for slot in (PP, L, R, PL_, PR, OO, OL, OR):
        stat_arrived(slot)
        if slot not in (L, R):
            arrived(AQ, slot)
            if slot != OO:
                arrived(AG, slot)
        key_slot(slot)

    place = lax.broadcasted_iota(jnp.int32, (rows, HEAD_DIM), 0)
    frame = (place >= 2 * cells).astype(jnp.int32)
    column = place - cells * (
        (place >= cells).astype(jnp.int32) + frame + (place >= 3 * cells).astype(jnp.int32)
    )
    own_0, own_1 = frame_len(TILE_SIDE * t), frame_len(TILE_SIDE * t + 1)
    live = column < jnp.where(frame == 1, own_1, own_0)

    @pl.loop(0, heads)
    def _(hd):
        whole = jnp.concatenate(convolve(AG, hd, True), axis=0)
        staged[2, hd] = jnp.where(live, key_acc[hd] * scale, 0.0).astype(BF16)
        staged[3, hd] = (jnp.where(live, value_acc[hd], 0.0) + whole).astype(BF16)

    store_all(2)
    store_all(3)
    for copy in sent:
        copy.wait_send()
    for slot in range(1, 9):
        stat_travel(slot).wait_send()
    for which in range(4):
        for hd in range(heads):
            store(which, hd).wait()


def shards(query_states, key_states, value_states, conv_weight, out_grad, tile_mask, clip_lengths):
    side_t, side_h, cells, channels = query_states.shape
    rows = side_t * side_h * cells
    padded = -(-rows // 128) * 128
    heads = channels // HEAD_DIM
    chunks = 2
    n_t, n_h = lax.axis_size("ta"), lax.axis_size("ha")
    flat = (rows, channels)
    any_space = pl.BlockSpec(memory_space=pl.ANY)
    outs = pl.pallas_call(
        functools.partial(kernel, heads, cells, rows, padded, n_t, n_h, chunks),
        out_shape=[jax.ShapeDtypeStruct(flat, BF16)] * 4,
        in_specs=[any_space] * 7,
        out_specs=[any_space] * 4,
        scratch_shapes=[
            pltpu.VMEM((4, 9, heads, padded, HEAD_DIM), BF16),
            pltpu.VMEM((9, heads, rows, padded), BF16),
            pltpu.VMEM((9, heads, rows, padded), F32),
            pltpu.VMEM((9, heads, rows, HEAD_DIM), F32),
            pltpu.VMEM((heads, rows, HEAD_DIM), F32),
            pltpu.VMEM((heads, rows, HEAD_DIM), F32),
            pltpu.VMEM((heads, rows, HEAD_DIM), F32),
            pltpu.VMEM((heads, rows, HEAD_DIM), F32),
            pltpu.VMEM((heads, rows, HEAD_DIM), F32),
            pltpu.VMEM((heads, rows, HEAD_DIM), F32),
            pltpu.VMEM((4, heads, rows, HEAD_DIM), BF16),
            pltpu.VMEM((9, 1, padded), F32),
            pltpu.VMEM((9, 1, padded), F32),
            pltpu.VMEM((padded, HEAD_DIM), F32),
            pltpu.VMEM((2 * heads, 1, padded), F32),
            pltpu.VMEM((9, 2 * heads, 1, padded), F32),
            pltpu.VMEM(conv_weight.shape, BF16),
            pltpu.VMEM((heads, conv_weight.shape[0], HEAD_DIM), F32),
            pltpu.VMEM((9, n_t, n_h), jnp.int32),
            pltpu.SMEM(clip_lengths.shape, jnp.int32),
            pltpu.SemaphoreType.DMA((4, heads)),
            pltpu.SemaphoreType.DMA((3,)),
            pltpu.SemaphoreType.DMA((4, heads)),
            pltpu.SemaphoreType.DMA((4, 9, chunks)),
            pltpu.SemaphoreType.DMA((4, 9, chunks)),
            pltpu.SemaphoreType.DMA((9,)),
            pltpu.SemaphoreType.DMA((9,)),
        ],
        compiler_params=pltpu.CompilerParams(
            collective_id=0, has_side_effects=True, vmem_limit_bytes=60 * 1024 * 1024
        ),
    )(
        query_states.reshape(flat),
        key_states.reshape(flat),
        value_states.reshape(flat),
        conv_weight,
        out_grad.reshape(flat),
        tile_mask.transpose(2, 0, 1),
        clip_lengths,
    )
    return tuple(out.reshape(query_states.shape) for out in outs)


def solution(mesh):
    tiled = P("ta", "ha", None, None)
    return jax.shard_map(
        shards,
        mesh=mesh,
        in_specs=(tiled, tiled, tiled, P(), tiled, P(), P()),
        out_specs=(tiled,) * 4,
        check_vma=False,
    )
```

```python
import functools
import math

import jax
import jax.numpy as jnp
from jax import lax
from jax.experimental import pallas as pl
from jax.experimental.pallas import tpu as pltpu
from jax.sharding import PartitionSpec as P

MESH = pl.DeviceIdType.MESH
HEAD_DIM = 128
TILE_SIDE = 2
F32 = jnp.float32
BF16 = jnp.bfloat16
BIG = 1e30
LOG2E = math.log2(math.e)

AK, AV, AQ, AG = 0, 1, 2, 3
OWN, L, R, PP, PL_, PR, OO, OL, OR = range(9)
GROUPS = ((OWN, PP), (OO,), (L, R), (PL_, PR), (OL, OR))
KEY_GROUPS = ((OWN, PP, OO), (L, R, PL_), (PR, OL, OR))
Y_FIRST = ((AV, 1), (AG, 1))
FWD_UNROLL = 3
KEY_UNROLL = 2

LAST = (((1,), (1,)), ((), ()))


def nt(a, b):
    return lax.dot_general(a, b, LAST, preferred_element_type=F32)


def nn(a, b):
    return jnp.dot(a, b, preferred_element_type=F32)


def kernel(
    heads, cells, rows, padded, n_t, n_h, chunks,
    q_hbm, k_hbm, v_hbm, w_hbm, g_hbm, mask_hbm, clip_hbm,
    out_hbm, dq_hbm, dk_hbm, dv_hbm,
    tiles, probs, dprobs, group_max, top, total, attn, delta, key_acc, value_acc, staged,
    bias, penalty, stat_mat, stat_out, stat_in, w_ref, wf_ref, mask_ref, clip_ref,
    load_sem, aux_sem, store_sem, send_sem, recv_sem, stat_send, stat_recv,
):
    scale = HEAD_DIM ** -0.5
    c2 = scale * LOG2E
    t = lax.axis_index("ta")
    h = lax.axis_index("ha")
    parity = lax.rem(t, 2)
    a_p = 1 - 2 * parity
    a_rows = (0, a_p, -a_p)
    b_cols = (0, -1, 1)
    t_rows = tuple(lax.rem(t + a + n_t, n_t) for a in a_rows)
    h_cols = tuple(lax.rem(h + b + n_h, n_h) for b in b_cols)
    flip = (0, 2, 1)
    hpc = heads // chunks
    has_row = (None, None, (t - a_p >= 0) & (t - a_p < n_t))
    has_col = (None, h > 0, h < n_h - 1)

    def exists(*slots):
        found = jnp.bool_(True)
        for slot in slots:
            for there in (has_row[slot // 3], has_col[slot % 3]):
                if there is not None:
                    found = found & there
        return found

    def load(arr, hd):
        src = (k_hbm, v_hbm, q_hbm, g_hbm)[arr]
        return pltpu.make_async_copy(
            src.at[:, pl.ds(hd * HEAD_DIM, HEAD_DIM)],
            tiles.at[arr, OWN, hd, pl.ds(0, rows)],
            load_sem.at[arr, hd],
        )

    for chunk in range(chunks):
        for arr in (AK, AV):
            for hd in range(chunk * hpc, (chunk + 1) * hpc):
                load(arr, hd).start()
    for arr in (AQ, AG):
        for hd in range(heads):
            load(arr, hd).start()
    aux = (
        pltpu.make_async_copy(mask_hbm, mask_ref, aux_sem.at[0]),
        pltpu.make_async_copy(clip_hbm, clip_ref, aux_sem.at[1]),
        pltpu.make_async_copy(w_hbm, w_ref, aux_sem.at[2]),
    )
    for copy in aux:
        copy.start()

    barrier = pltpu.get_barrier_semaphore()
    for slot in range(1, 9):
        @pl.when(exists(slot))
        def _():
            pl.semaphore_signal(
                barrier, inc=1, device_id=(t_rows[slot // 3], h_cols[slot % 3]), device_id_type=MESH
            )
    near_t = 2 + has_row[2].astype(jnp.int32)
    near_h = 1 + has_col[1].astype(jnp.int32) + has_col[2].astype(jnp.int32)
    pl.semaphore_wait(barrier, near_t * near_h - 1)

    def travel(arr, src_slot, to, chunk):
        row, col = src_slot // 3, src_slot % 3
        if to in (L, R):
            dst_slot = 3 * row + flip[to]
            device = (t, h_cols[to])
        else:
            dst_slot = to + col
            device = (t_rows[to // 3], h)
        part = (pl.ds(chunk * hpc, hpc), pl.ds(0, rows))
        return pltpu.make_async_remote_copy(
            src_ref=tiles.at[(arr, src_slot) + part],
            dst_ref=tiles.at[(arr, dst_slot) + part],
            send_sem=send_sem.at[arr, dst_slot, chunk],
            recv_sem=recv_sem.at[arr, dst_slot, chunk],
            device_id=device,
            device_id_type=MESH,
        )

    sent = []

    def send(arr, src_slot, targets):
        for chunk in range(chunks):
            send_chunk(arr, src_slot, targets, chunk)

    def send_chunk(arr, src_slot, targets, chunk):
        for to in targets:
            sent.append((arr, src_slot, to, chunk))

            @pl.when(exists(src_slot, to))
            def _():
                travel(arr, src_slot, to, chunk).start()

    def arrived_chunk(arr, slot, chunk):
        part = (pl.ds(chunk * hpc, hpc), pl.ds(0, rows))
        place = tiles.at[(arr, slot) + part]

        @pl.when(exists(slot))
        def _():
            pltpu.make_async_remote_copy(
                src_ref=place, dst_ref=place,
                send_sem=send_sem.at[arr, slot, chunk], recv_sem=recv_sem.at[arr, slot, chunk],
                device_id=(t_rows[1], h), device_id_type=MESH,
            ).wait_recv()

    def arrived(arr, slot):
        for chunk in range(chunks):
            arrived_chunk(arr, slot, chunk)

    for chunk in range(chunks):
        for arr in (AK, AV):
            for hd in range(chunk * hpc, (chunk + 1) * hpc):
                load(arr, hd).wait()
            send_chunk(arr, OWN, (OO, L, R, PP), chunk)
    for arr in (AQ, AG):
        for hd in range(heads):
            load(arr, hd).wait()
        send(arr, OWN, (PP,))

    def pass_sides(arr, chunk):
        for side in (L, R):
            arrived_chunk(arr, side, chunk)
            send_chunk(arr, side, (PP,) if (arr, chunk) in Y_FIRST else (OO, PP), chunk)

    def pass_other(arr, chunk):
        arrived_chunk(arr, OO, chunk)
        if (arr, chunk) in Y_FIRST:
            send_chunk(arr, OO, (L, R), chunk)

    @pl.loop(0, 4 * 9)
    def _(i):
        tiles[i // 9, i % 9, :, pl.ds(rows, padded - rows), :] = jnp.zeros(
            (heads, padded - rows, HEAD_DIM), BF16
        )

    for slot in range(1, 9):
        if slot != PP:
            @pl.when(jnp.logical_not(exists(slot)))
            def _():
                stat_in[slot] = jnp.zeros(stat_in.shape[1:], F32)

                @pl.loop(0, 4 * heads)
                def _(i):
                    tiles[i // heads, slot, i % heads, pl.ds(0, rows), :] = jnp.zeros(
                        (rows, HEAD_DIM), BF16
                    )

    for copy in aux:
        copy.wait()

    lane = lax.broadcasted_iota(jnp.int32, (1, padded), 1)
    tile_frame = (lane >= 2 * cells).astype(jnp.int32)
    column = lane - cells * (
        (lane >= cells).astype(jnp.int32) + tile_frame + (lane >= 3 * cells).astype(jnp.int32)
    )
    shape = mask_ref.shape[1:]
    it = lax.broadcasted_iota(jnp.int32, shape, 0)
    ih = lax.broadcasted_iota(jnp.int32, shape, 1)

    def frame_len(frame):
        live = clip_ref[jnp.clip(frame, 0, TILE_SIDE * n_t - 1)]
        return jnp.where((frame >= 0) & (frame < TILE_SIDE * n_t), live, 0)

    def entry(index, at_t, at_h):
        here = (it == at_t) & (ih == at_h)
        picked = jnp.where(here, mask_ref[index], 0).astype(F32)
        return jnp.sum(picked, axis=(0, 1), keepdims=True)

    for slot in range(9):
        a, b = a_rows[slot // 3], b_cols[slot % 3]
        index = 3 * (a + 1) + (b + 1)
        first = TILE_SIDE * (t + a)
        len_0, len_1 = frame_len(first), frame_len(first + 1)
        inside = ((h + b >= 0) & (h + b < n_h)).astype(jnp.int32)
        live = jnp.where(tile_frame == 1, len_1 * inside, len_0 * inside)
        seen = (column < live) & (lane < rows)
        keep = jnp.where(seen, entry(index, t, h), 0.0)
        bias[slot] = jnp.where(keep > 0.5, 0.0, -BIG)
        facing = entry(8 - index, t + a, h + b)
        penalty[slot] = jnp.where((lane < rows), jnp.where(facing > 0.5, 0.0, BIG), BIG)

    def forward_group(group, chunk):
        slots = GROUPS[group]

        @pl.loop(chunk * hpc, (chunk + 1) * hpc, unroll=FWD_UNROLL)
        def _(hd):
            q = tiles[AQ, OWN, hd, pl.ds(0, rows), :]
            g = tiles[AG, OWN, hd, pl.ds(0, rows), :]
            scores = [nt(q, tiles[AK, slot, hd]) + bias[slot] for slot in slots]
            m = jnp.max(functools.reduce(jnp.maximum, scores), axis=-1, keepdims=True)
            ps = [jnp.exp2((s - m) * c2) for s in scores]
            row_sum = jnp.sum(functools.reduce(jnp.add, ps), axis=-1, keepdims=True)
            ps = [p.astype(BF16) for p in ps]
            for slot, p in zip(slots, ps, strict=True):
                probs[slot, hd] = p
                dprobs[slot, hd] = nt(g, tiles[AV, slot, hd])
            part = nn(
                jnp.concatenate(ps, axis=1),
                jnp.concatenate([tiles[AV, slot, hd] for slot in slots], axis=0),
            )
            m = jnp.broadcast_to(m, (rows, HEAD_DIM))
            group_max[group, hd] = m
            if group == 0:
                top[hd] = m
                total[hd] = jnp.broadcast_to(row_sum, (rows, HEAD_DIM))
                attn[hd] = part
            else:
                old = top[hd]
                new = jnp.maximum(old, m)
                keep_old = jnp.exp2((old - new) * c2)
                keep_new = jnp.exp2((m - new) * c2)
                top[hd] = new
                total[hd] = total[hd] * keep_old + row_sum * keep_new
                attn[hd] = attn[hd] * keep_old + part * keep_new

    def key_group(slots, beside=None):
        @pl.loop(0, heads, unroll=KEY_UNROLL)
        def _(hd):
            k = tiles[AK, OWN, hd, pl.ds(0, rows), :]
            v = tiles[AV, OWN, hd, pl.ds(0, rows), :]
            ps, dss = [], []
            for slot in slots:
                log_total = stat_in[slot, 2 * hd] + penalty[slot]
                p = jnp.exp2(nt(k, tiles[AQ, slot, hd]) * c2 - log_total)
                ps.append(p.astype(BF16))
                ds = p * (nt(v, tiles[AG, slot, hd]) - stat_in[slot, 2 * hd + 1])
                dss.append(ds.astype(BF16))
            for acc, sides, arr in ((value_acc, ps, AG), (key_acc, dss, AQ)):
                part = nn(
                    jnp.concatenate(sides, axis=1),
                    jnp.concatenate([tiles[arr, slot, hd] for slot in slots], axis=0),
                )
                if slots[0] == OWN:
                    acc[hd] = part
                else:
                    acc[hd] += part
            if beside is not None:
                beside(hd)

    def convolve(arr, hd, flipped):
        r_minus, r_plus = 2 - parity, 1 + parity
        in_t = ((t > 0).astype(F32), None, None, (t < n_t - 1).astype(F32))
        in_h = ((h > 0).astype(F32), None, None, (h < n_h - 1).astype(F32))
        source = {}
        for big_i in range(4):
            row = (r_minus, 0, 0, r_plus)[big_i]
            for big_j in range(4):
                col = (1, 0, 0, 2)[big_j]
                i, j = (1, 0, 1, 0)[big_i], (1, 0, 1, 0)[big_j]
                whole = tiles[arr, 3 * row + col, hd, pl.ds(0, rows), :].astype(F32)
                start = (2 * i + j) * cells
                piece = whole[start:start + cells]
                for factor in (in_t[big_i], in_h[big_j]):
                    if factor is not None:
                        piece = piece * factor
                source[big_i, big_j] = piece
        place = lax.broadcasted_iota(jnp.int32, (cells, HEAD_DIM), 0)
        pieces = []
        for i in range(2):
            for j in range(2):
                sums = []
                for dw in range(3):
                    acc = None
                    for dt in range(3):
                        for dh in range(3):
                            o = 9 * dt + 3 * dh + dw
                            o = 26 - o if flipped else o
                            term = source[i + dt, j + dh] * wf_ref[hd, pl.ds(o, 1), :]
                            acc = term if acc is None else acc + term
                    sums.append(acc)
                before = jnp.where(place == 0, 0.0, pltpu.roll(sums[0], 1, 0))
                after = jnp.where(place == cells - 1, 0.0, pltpu.roll(sums[2], cells - 1, 0))
                pieces.append(sums[1] + before + after)
        return pieces

    def store(which, hd):
        dst = (out_hbm, dq_hbm, dk_hbm, dv_hbm)[which]
        return pltpu.make_async_copy(
            staged.at[which, hd],
            dst.at[:, pl.ds(hd * HEAD_DIM, HEAD_DIM)],
            store_sem.at[which, hd],
        )

    def store_all(which):
        for hd in range(heads):
            store(which, hd).start()

    for hd in range(heads):
        wf_ref[hd] = w_ref[:, hd * HEAD_DIM:(hd + 1) * HEAD_DIM].astype(F32)

    arrived(AK, PP)
    arrived(AV, PP)
    for chunk in range(chunks):
        forward_group(0, chunk)
    last = chunks - 1
    for chunk in range(chunks):
        if chunk == last:
            send(AQ, OWN, (L, R))
        for arr in (AK, AV):
            pass_sides(arr, chunk)
        if chunk == last:
            send(AG, OWN, (OO,))
        else:
            for part in range(chunks):
                for arr in (AK, AV):
                    pass_other(arr, part)
                forward_group(1, part)
        for arr in (AK, AV):
            for slot in (PL_, PR):
                arrived_chunk(arr, slot, chunk)
        forward_group(2, chunk)
        forward_group(3, chunk)
    for chunk in range(chunks):
        for arr in (AK, AV):
            for slot in (OL, OR):
                arrived_chunk(arr, slot, chunk)
        forward_group(4, chunk)

    stat_mat[...] = jnp.zeros_like(stat_mat)

    @pl.loop(0, heads)
    def _(hd):
        g = tiles[AG, OWN, hd, pl.ds(0, rows), :].astype(F32)
        sums = total[hd]
        inverse = 1.0 / sums
        d = jnp.sum(g * attn[hd], axis=-1, keepdims=True) * inverse
        delta[hd] = d
        log_total = top[hd] * c2 + jnp.log(sums) * LOG2E
        lanes = lax.broadcasted_iota(jnp.int32, (rows, HEAD_DIM), 1)
        stat_mat[pl.ds(0, rows), :] = jnp.where(
            lanes == 2 * hd, log_total, jnp.where(lanes == 2 * hd + 1, d, stat_mat[pl.ds(0, rows), :])
        )

    as_rows = stat_mat[...].T
    for i in range(2 * heads):
        stat_out[i] = as_rows[i:i + 1]
        stat_in[OWN, i] = as_rows[i:i + 1]

    def stat_travel(slot):
        row, col = slot // 3, slot % 3
        dst_slot = 3 * row + flip[col]
        return pltpu.make_async_remote_copy(
            src_ref=stat_out,
            dst_ref=stat_in.at[dst_slot],
            send_sem=stat_send.at[dst_slot],
            recv_sem=stat_recv.at[dst_slot],
            device_id=(t_rows[row], h_cols[col]),
            device_id_type=MESH,
        )

    def stat_arrived(slot):
        @pl.when(exists(slot))
        def _():
            pltpu.make_async_remote_copy(
                src_ref=stat_in.at[slot], dst_ref=stat_in.at[slot],
                send_sem=stat_send.at[slot], recv_sem=stat_recv.at[slot],
                device_id=(t_rows[1], h), device_id_type=MESH,
            ).wait_recv()

    for slot in (PP, L, R, OO, PL_, PR, OL, OR):
        @pl.when(exists(slot))
        def _():
            stat_travel(slot).start()

    send(AQ, OWN, (OO,))
    send(AG, OWN, (L, R))
    for chunk in range(chunks):
        pass_sides(AQ, chunk)
    for chunk in range(chunks):
        pass_other(AG, chunk)

    @pl.loop(0, heads)
    def _(hd):
        d = delta[hd]
        d = jnp.concatenate([d, d], axis=1)
        best = top[hd]

        acc = None
        for group, slots in enumerate(GROUPS):
            sides = [
                probs[slot, hd] * (dprobs[slot, hd] - d).astype(BF16) for slot in slots
            ]
            part = nn(
                jnp.concatenate(sides, axis=1),
                jnp.concatenate([tiles[AK, slot, hd] for slot in slots], axis=0),
            ) * jnp.exp2((group_max[group, hd] - best) * c2)
            acc = part if acc is None else acc + part
        staged[1, hd] = (acc * (scale / total[hd])).astype(BF16)

    store_all(1)

    place = lax.broadcasted_iota(jnp.int32, (rows, HEAD_DIM), 0)
    frame = (place >= 2 * cells).astype(jnp.int32)
    column = place - cells * (
        (place >= cells).astype(jnp.int32) + frame + (place >= 3 * cells).astype(jnp.int32)
    )
    own_0, own_1 = frame_len(TILE_SIDE * t), frame_len(TILE_SIDE * t + 1)
    live = column < jnp.where(frame == 1, own_1, own_0)

    def finish_out(hd):
        whole = jnp.concatenate(convolve(AV, hd, False), axis=0)
        staged[0, hd] = (attn[hd] / total[hd] + whole).astype(BF16)

    def finish_grads(hd):
        whole = jnp.concatenate(convolve(AG, hd, True), axis=0)
        staged[2, hd] = jnp.where(live, key_acc[hd] * scale, 0.0).astype(BF16)
        staged[3, hd] = (jnp.where(live, value_acc[hd], 0.0) + whole).astype(BF16)

    for slot in (PP, OO):
        stat_arrived(slot)
        arrived(AQ, slot)
    arrived(AG, PP)
    key_group(KEY_GROUPS[0], finish_out)
    store_all(0)
    for chunk in range(chunks):
        pass_sides(AG, chunk)
    for slot in (L, R, PL_):
        stat_arrived(slot)
    arrived(AQ, PL_)
    arrived(AG, PL_)
    key_group(KEY_GROUPS[1])
    for slot in KEY_GROUPS[2]:
        stat_arrived(slot)
        arrived(AQ, slot)
        arrived(AG, slot)
    key_group(KEY_GROUPS[2], finish_grads)
    store_all(2)
    store_all(3)
    for arr, src_slot, to, chunk in sent:
        @pl.when(exists(src_slot, to))
        def _():
            travel(arr, src_slot, to, chunk).wait_send()

    for slot in range(1, 9):
        @pl.when(exists(slot))
        def _():
            stat_travel(slot).wait_send()

    for which in range(4):
        for hd in range(heads):
            store(which, hd).wait()


def hand_over(*refs):
    ins, outs, (held, in_sem, out_sem) = refs[:4], refs[4:8], refs[8:]
    arrive = [pltpu.make_async_copy(ins[i], held.at[i], in_sem.at[i]) for i in range(4)]
    leave = [pltpu.make_async_copy(held.at[i], outs[i], out_sem.at[i]) for i in range(4)]
    for copy in arrive:
        copy.start()
    for first, then in zip(arrive, leave, strict=True):
        first.wait()
        then.start()
    for copy in leave:
        copy.wait()


def shards(query_states, key_states, value_states, conv_weight, out_grad, tile_mask, clip_lengths):
    side_t, side_h, cells, channels = query_states.shape
    rows = side_t * side_h * cells
    padded = -(-rows // 128) * 128
    heads = channels // HEAD_DIM
    chunks = 2
    n_t, n_h = lax.axis_size("ta"), lax.axis_size("ha")
    flat = (rows, channels)
    any_space = pl.BlockSpec(memory_space=pl.ANY)
    outs = pl.pallas_call(
        functools.partial(kernel, heads, cells, rows, padded, n_t, n_h, chunks),
        out_shape=[jax.ShapeDtypeStruct(flat, BF16)] * 4,
        in_specs=[any_space] * 7,
        out_specs=[any_space] * 4,
        scratch_shapes=[
            pltpu.VMEM((4, 9, heads, padded, HEAD_DIM), BF16),
            pltpu.VMEM((9, heads, rows, padded), BF16),
            pltpu.VMEM((9, heads, rows, padded), F32),
            pltpu.VMEM((len(GROUPS), heads, rows, HEAD_DIM), F32),
            pltpu.VMEM((heads, rows, HEAD_DIM), F32),
            pltpu.VMEM((heads, rows, HEAD_DIM), F32),
            pltpu.VMEM((heads, rows, HEAD_DIM), F32),
            pltpu.VMEM((heads, rows, HEAD_DIM), F32),
            pltpu.VMEM((heads, rows, HEAD_DIM), F32),
            pltpu.VMEM((heads, rows, HEAD_DIM), F32),
            pltpu.VMEM((4, heads, rows, HEAD_DIM), BF16),
            pltpu.VMEM((9, 1, padded), F32),
            pltpu.VMEM((9, 1, padded), F32),
            pltpu.VMEM((padded, HEAD_DIM), F32),
            pltpu.VMEM((2 * heads, 1, padded), F32),
            pltpu.VMEM((9, 2 * heads, 1, padded), F32),
            pltpu.VMEM(conv_weight.shape, BF16),
            pltpu.VMEM((heads, conv_weight.shape[0], HEAD_DIM), F32),
            pltpu.VMEM((9, n_t, n_h), jnp.int32),
            pltpu.SMEM(clip_lengths.shape, jnp.int32),
            pltpu.SemaphoreType.DMA((4, heads)),
            pltpu.SemaphoreType.DMA((3,)),
            pltpu.SemaphoreType.DMA((4, heads)),
            pltpu.SemaphoreType.DMA((4, 9, chunks)),
            pltpu.SemaphoreType.DMA((4, 9, chunks)),
            pltpu.SemaphoreType.DMA((9,)),
            pltpu.SemaphoreType.DMA((9,)),
        ],
        compiler_params=pltpu.CompilerParams(
            collective_id=0, has_side_effects=True, vmem_limit_bytes=60 * 1024 * 1024
        ),
    )(
        query_states.reshape(flat),
        key_states.reshape(flat),
        value_states.reshape(flat),
        conv_weight,
        out_grad.reshape(flat),
        tile_mask.transpose(2, 0, 1),
        clip_lengths,
    )
    outs = pl.pallas_call(
        hand_over,
        out_shape=[jax.ShapeDtypeStruct(flat, BF16)] * 4,
        in_specs=[any_space] * 4,
        out_specs=[any_space] * 4,
        scratch_shapes=[
            pltpu.VMEM((4,) + flat, BF16),
            pltpu.SemaphoreType.DMA((4,)),
            pltpu.SemaphoreType.DMA((4,)),
        ],
    )(*outs)
    return tuple(out.reshape(query_states.shape) for out in outs)


def solution(mesh):
    tiled = P("ta", "ha", None, None)
    return jax.shard_map(
        shards,
        mesh=mesh,
        in_specs=(tiled, tiled, tiled, P(), tiled, P(), P()),
        out_specs=(tiled,) * 4,
        check_vma=False,
    )
```

```python
import functools
import math

import jax
import jax.numpy as jnp
from jax import lax
from jax.experimental import pallas as pl
from jax.experimental.pallas import tpu as pltpu
from jax.sharding import PartitionSpec as P

MESH = pl.DeviceIdType.MESH
HEAD_DIM = 128
TILE_SIDE = 2
F32 = jnp.float32
BF16 = jnp.bfloat16
BIG = 1e30
LOG2E = math.log2(math.e)

AK, AV, AQ, AG = 0, 1, 2, 3
OWN, L, R, PP, PL_, PR, OO, OL, OR = range(9)
GROUPS = ((OWN, PP), (OO,), (R, PR, OR), (L, PL_, OL))
KEY_GROUPS = ((OWN, PP, OO), (R, PR, OR), (L, PL_, OL))
Y_FIRST = ((AV, 1), (AG, 1))
FWD_UNROLL = 3
KEY_UNROLL = 3
Z_CHIPS = 12

LAST = (((1,), (1,)), ((), ()))


def nt(a, b):
    return lax.dot_general(a, b, LAST, preferred_element_type=F32)


def nn(a, b):
    return jnp.dot(a, b, preferred_element_type=F32)


def kernel(
    heads, cells, rows, padded, n_t, n_h, chunks,
    q_hbm, k_hbm, v_hbm, w_hbm, g_hbm, mask_hbm, clip_hbm,
    out_hbm, dq_hbm, dk_hbm, dv_hbm,
    tiles, probs, dprobs, group_max, top, total, attn, delta, key_acc, value_acc, staged,
    bias, penalty, stat_mat, stat_out, stat_in, w_ref, wf_ref, mask_ref, clip_ref,
    load_sem, aux_sem, store_sem, send_sem, recv_sem, stat_send, stat_recv,
):
    scale = HEAD_DIM ** -0.5
    c2 = scale * LOG2E
    t = lax.axis_index("ta")
    h = lax.axis_index("ha")
    parity = lax.rem(t, 2)
    a_p = 1 - 2 * parity
    a_rows = (0, a_p, -a_p)
    b_cols = (0, -1, 1)
    t_rows = tuple(lax.rem(t + a + n_t, n_t) for a in a_rows)
    h_cols = tuple(lax.rem(h + b + n_h, n_h) for b in b_cols)
    flip = (0, 2, 1)
    hpc = heads // chunks
    has_row = (None, None, (t - a_p >= 0) & (t - a_p < n_t))
    has_col = (None, h > 0, h < n_h - 1)

    late_left = (h > 0) & (lax.rem(h, Z_CHIPS) == 0)
    to_early = (h < n_h - 1) & (lax.rem(h, Z_CHIPS) == Z_CHIPS - 1)

    def exists(*slots, also=None):
        found = jnp.bool_(True) if also is None else also
        for slot in slots:
            for there in (has_row[slot // 3], has_col[slot % 3]):
                if there is not None:
                    found = found & there
        return found

    def load(arr, hd):
        src = (k_hbm, v_hbm, q_hbm, g_hbm)[arr]
        return pltpu.make_async_copy(
            src.at[:, pl.ds(hd * HEAD_DIM, HEAD_DIM)],
            tiles.at[arr, OWN, hd, pl.ds(0, rows)],
            load_sem.at[arr, hd],
        )

    for chunk in range(chunks):
        for arr in (AK, AV):
            for hd in range(chunk * hpc, (chunk + 1) * hpc):
                load(arr, hd).start()
    for arr in (AQ, AG):
        for hd in range(heads):
            load(arr, hd).start()
    aux = (
        pltpu.make_async_copy(mask_hbm, mask_ref, aux_sem.at[0]),
        pltpu.make_async_copy(clip_hbm, clip_ref, aux_sem.at[1]),
        pltpu.make_async_copy(w_hbm, w_ref, aux_sem.at[2]),
    )
    for copy in aux:
        copy.start()

    barrier = pltpu.get_barrier_semaphore()
    for slot in range(1, 9):
        @pl.when(exists(slot))
        def _():
            pl.semaphore_signal(
                barrier, inc=1, device_id=(t_rows[slot // 3], h_cols[slot % 3]), device_id_type=MESH
            )
    near_t = 2 + has_row[2].astype(jnp.int32)
    near_h = 1 + has_col[1].astype(jnp.int32) + has_col[2].astype(jnp.int32)
    pl.semaphore_wait(barrier, near_t * near_h - 1)

    def travel(arr, src_slot, to, chunk):
        row, col = src_slot // 3, src_slot % 3
        if to in (L, R):
            dst_slot = 3 * row + flip[to]
            device = (t, h_cols[to])
        else:
            dst_slot = to + col
            device = (t_rows[to // 3], h)
        part = (pl.ds(chunk * hpc, hpc), pl.ds(0, rows))
        return pltpu.make_async_remote_copy(
            src_ref=tiles.at[(arr, src_slot) + part],
            dst_ref=tiles.at[(arr, dst_slot) + part],
            send_sem=send_sem.at[arr, 0 if (src_slot, to) == (OO, R) else dst_slot, chunk],
            recv_sem=recv_sem.at[arr, dst_slot, chunk],
            device_id=device,
            device_id_type=MESH,
        )

    sent = []

    def send(arr, src_slot, targets):
        for chunk in range(chunks):
            send_chunk(arr, src_slot, targets, chunk)

    def send_chunk(arr, src_slot, targets, chunk, also=None):
        for to in targets:
            sent.append((arr, src_slot, to, chunk, also))

            @pl.when(exists(src_slot, to, also=also))
            def _():
                travel(arr, src_slot, to, chunk).start()

    def arrived_chunk(arr, slot, chunk):
        part = (pl.ds(chunk * hpc, hpc), pl.ds(0, rows))
        place = tiles.at[(arr, slot) + part]

        @pl.when(exists(slot))
        def _():
            pltpu.make_async_remote_copy(
                src_ref=place, dst_ref=place,
                send_sem=send_sem.at[arr, slot, chunk], recv_sem=recv_sem.at[arr, slot, chunk],
                device_id=(t_rows[1], h), device_id_type=MESH,
            ).wait_recv()

    def arrived(arr, slot):
        for chunk in range(chunks):
            arrived_chunk(arr, slot, chunk)

    for chunk in range(chunks):
        for arr in (AK, AV):
            for hd in range(chunk * hpc, (chunk + 1) * hpc):
                load(arr, hd).wait()
            send_chunk(arr, OWN, (OO, L, R, PP), chunk)
    for arr in (AQ, AG):
        for hd in range(heads):
            load(arr, hd).wait()
        send(arr, OWN, (PP,))

    def pass_side(arr, side, chunk):
        arrived_chunk(arr, side, chunk)
        send_chunk(arr, side, (PP,), chunk)
        if (arr, chunk) not in Y_FIRST:
            send_chunk(arr, side, (OO,), chunk)
        elif side == L:
            send_chunk(arr, side, (OO,), chunk, late_left)

    def pass_right(*parts):
        for arr, chunk in parts:
            pass_side(arr, R, chunk)

    def pass_left(late, *parts):
        before = len(sent)

        @pl.when(late_left if late else jnp.logical_not(late_left))
        def _():
            for arr, chunk in parts:
                pass_side(arr, L, chunk)

        if late:
            del sent[before:]

    def pass_other(arr, chunk):
        arrived_chunk(arr, OO, chunk)
        if (arr, chunk) in Y_FIRST:
            send_chunk(arr, OO, (L,), chunk)
            send_chunk(arr, OO, (R,), chunk, jnp.logical_not(to_early))

    @pl.loop(0, 4 * 9)
    def _(i):
        tiles[i // 9, i % 9, :, pl.ds(rows, padded - rows), :] = jnp.zeros(
            (heads, padded - rows, HEAD_DIM), BF16
        )

    for slot in range(1, 9):
        if slot != PP:
            @pl.when(jnp.logical_not(exists(slot)))
            def _():
                stat_in[slot] = jnp.zeros(stat_in.shape[1:], F32)

                @pl.loop(0, 4 * heads)
                def _(i):
                    tiles[i // heads, slot, i % heads, pl.ds(0, rows), :] = jnp.zeros(
                        (rows, HEAD_DIM), BF16
                    )

    for copy in aux:
        copy.wait()

    lane = lax.broadcasted_iota(jnp.int32, (1, padded), 1)
    tile_frame = (lane >= 2 * cells).astype(jnp.int32)
    column = lane - cells * (
        (lane >= cells).astype(jnp.int32) + tile_frame + (lane >= 3 * cells).astype(jnp.int32)
    )
    shape = mask_ref.shape[1:]
    it = lax.broadcasted_iota(jnp.int32, shape, 0)
    ih = lax.broadcasted_iota(jnp.int32, shape, 1)

    def frame_len(frame):
        live = clip_ref[jnp.clip(frame, 0, TILE_SIDE * n_t - 1)]
        return jnp.where((frame >= 0) & (frame < TILE_SIDE * n_t), live, 0)

    def entry(index, at_t, at_h):
        here = (it == at_t) & (ih == at_h)
        picked = jnp.where(here, mask_ref[index], 0).astype(F32)
        return jnp.sum(picked, axis=(0, 1), keepdims=True)

    for slot in range(9):
        a, b = a_rows[slot // 3], b_cols[slot % 3]
        index = 3 * (a + 1) + (b + 1)
        first = TILE_SIDE * (t + a)
        len_0, len_1 = frame_len(first), frame_len(first + 1)
        inside = ((h + b >= 0) & (h + b < n_h)).astype(jnp.int32)
        live = jnp.where(tile_frame == 1, len_1 * inside, len_0 * inside)
        seen = (column < live) & (lane < rows)
        keep = jnp.where(seen, entry(index, t, h), 0.0)
        bias[slot] = jnp.where(keep > 0.5, 0.0, -BIG)
        facing = entry(8 - index, t + a, h + b)
        penalty[slot] = jnp.where((lane < rows), jnp.where(facing > 0.5, 0.0, BIG), BIG)

    def forward_group(group, chunk):
        slots = GROUPS[group]

        @pl.loop(chunk * hpc, (chunk + 1) * hpc, unroll=FWD_UNROLL)
        def _(hd):
            q = tiles[AQ, OWN, hd, pl.ds(0, rows), :]
            g = tiles[AG, OWN, hd, pl.ds(0, rows), :]
            scores = [nt(q, tiles[AK, slot, hd]) + bias[slot] for slot in slots]
            m = jnp.max(functools.reduce(jnp.maximum, scores), axis=-1, keepdims=True)
            ps = [jnp.exp2((s - m) * c2) for s in scores]
            row_sum = jnp.sum(functools.reduce(jnp.add, ps), axis=-1, keepdims=True)
            ps = [p.astype(BF16) for p in ps]
            for slot, p in zip(slots, ps, strict=True):
                probs[slot, hd] = p
                dprobs[slot, hd] = nt(g, tiles[AV, slot, hd])
            part = nn(
                jnp.concatenate(ps, axis=1),
                jnp.concatenate([tiles[AV, slot, hd] for slot in slots], axis=0),
            )
            m = jnp.broadcast_to(m, (rows, HEAD_DIM))
            group_max[group, hd] = m
            if group == 0:
                top[hd] = m
                total[hd] = jnp.broadcast_to(row_sum, (rows, HEAD_DIM))
                attn[hd] = part
            else:
                old = top[hd]
                new = jnp.maximum(old, m)
                keep_old = jnp.exp2((old - new) * c2)
                keep_new = jnp.exp2((m - new) * c2)
                top[hd] = new
                total[hd] = total[hd] * keep_old + row_sum * keep_new
                attn[hd] = attn[hd] * keep_old + part * keep_new

    def key_group(slots, chunk, beside=None):
        @pl.loop(chunk * hpc, (chunk + 1) * hpc, unroll=KEY_UNROLL)
        def _(hd):
            k = tiles[AK, OWN, hd, pl.ds(0, rows), :]
            v = tiles[AV, OWN, hd, pl.ds(0, rows), :]
            ps, dss = [], []
            for slot in slots:
                log_total = stat_in[slot, 2 * hd] + penalty[slot]
                p = jnp.exp2(nt(k, tiles[AQ, slot, hd]) * c2 - log_total)
                ps.append(p.astype(BF16))
                ds = p * (nt(v, tiles[AG, slot, hd]) - stat_in[slot, 2 * hd + 1])
                dss.append(ds.astype(BF16))
            for acc, sides, arr in ((value_acc, ps, AG), (key_acc, dss, AQ)):
                part = nn(
                    jnp.concatenate(sides, axis=1),
                    jnp.concatenate([tiles[arr, slot, hd] for slot in slots], axis=0),
                )
                if slots[0] == OWN:
                    acc[hd] = part
                else:
                    acc[hd] += part
            if beside is not None:
                beside(hd)

    def convolve(arr, hd, flipped):
        r_minus, r_plus = 2 - parity, 1 + parity
        in_t = ((t > 0).astype(F32), None, None, (t < n_t - 1).astype(F32))
        in_h = ((h > 0).astype(F32), None, None, (h < n_h - 1).astype(F32))
        source = {}
        for big_i in range(4):
            row = (r_minus, 0, 0, r_plus)[big_i]
            for big_j in range(4):
                col = (1, 0, 0, 2)[big_j]
                i, j = (1, 0, 1, 0)[big_i], (1, 0, 1, 0)[big_j]
                whole = tiles[arr, 3 * row + col, hd, pl.ds(0, rows), :].astype(F32)
                start = (2 * i + j) * cells
                piece = whole[start:start + cells]
                for factor in (in_t[big_i], in_h[big_j]):
                    if factor is not None:
                        piece = piece * factor
                source[big_i, big_j] = piece
        place = lax.broadcasted_iota(jnp.int32, (cells, HEAD_DIM), 0)
        pieces = []
        for i in range(2):
            for j in range(2):
                sums = []
                for dw in range(3):
                    acc = None
                    for dt in range(3):
                        for dh in range(3):
                            o = 9 * dt + 3 * dh + dw
                            o = 26 - o if flipped else o
                            term = source[i + dt, j + dh] * wf_ref[hd, pl.ds(o, 1), :]
                            acc = term if acc is None else acc + term
                    sums.append(acc)
                before = jnp.where(place == 0, 0.0, pltpu.roll(sums[0], 1, 0))
                after = jnp.where(place == cells - 1, 0.0, pltpu.roll(sums[2], cells - 1, 0))
                pieces.append(sums[1] + before + after)
        return pieces

    def store(which, hd):
        dst = (out_hbm, dq_hbm, dk_hbm, dv_hbm)[which]
        return pltpu.make_async_copy(
            staged.at[which, hd],
            dst.at[:, pl.ds(hd * HEAD_DIM, HEAD_DIM)],
            store_sem.at[which, hd],
        )

    def store_all(which):
        for hd in range(heads):
            store(which, hd).start()

    for hd in range(heads):
        wf_ref[hd] = w_ref[:, hd * HEAD_DIM:(hd + 1) * HEAD_DIM].astype(F32)

    arrived(AK, PP)
    arrived(AV, PP)
    for chunk in range(chunks):
        forward_group(0, chunk)
    first, second = ((AK, 0), (AV, 0)), ((AK, 1), (AV, 1))
    pass_right(*first)
    pass_left(False, *first)
    for arr, chunk in first:
        pass_other(arr, chunk)
    forward_group(1, 0)
    for arr, chunk in second:
        pass_other(arr, chunk)
    for chunk in range(chunks):
        for arr in (AQ, AG):
            send_chunk(arr, OWN, (L, R), chunk)
    forward_group(1, 1)

    def arrived_all(arrs, slots, chunk):
        for slot in slots:
            for arr in arrs:
                arrived_chunk(arr, slot, chunk)

    arrived_all((AK, AV), (PR, OR), 0)
    forward_group(2, 0)
    pass_right(*second)
    pass_left(False, *second)
    for chunk in range(chunks):
        for arr in (AQ, AG):
            send_chunk(arr, OWN, (OO,), chunk)
    arrived_all((AK, AV), (PR, OR), 1)
    forward_group(2, 1)
    pass_left(True, *first, second[0])
    arrived_all((AK, AV), (PL_, OL), 0)
    forward_group(3, 0)
    pass_left(True, second[1])
    arrived_all((AK, AV), (PL_, OL), 1)
    forward_group(3, 1)

    stat_mat[...] = jnp.zeros_like(stat_mat)

    @pl.loop(0, heads)
    def _(hd):
        g = tiles[AG, OWN, hd, pl.ds(0, rows), :].astype(F32)
        sums = total[hd]
        inverse = 1.0 / sums
        d = jnp.sum(g * attn[hd], axis=-1, keepdims=True) * inverse
        delta[hd] = d
        log_total = top[hd] * c2 + jnp.log(sums) * LOG2E
        lanes = lax.broadcasted_iota(jnp.int32, (rows, HEAD_DIM), 1)
        stat_mat[pl.ds(0, rows), :] = jnp.where(
            lanes == 2 * hd, log_total, jnp.where(lanes == 2 * hd + 1, d, stat_mat[pl.ds(0, rows), :])
        )

    as_rows = stat_mat[...].T
    for i in range(2 * heads):
        stat_out[i] = as_rows[i:i + 1]
        stat_in[OWN, i] = as_rows[i:i + 1]

    def stat_travel(slot):
        row, col = slot // 3, slot % 3
        dst_slot = 3 * row + flip[col]
        return pltpu.make_async_remote_copy(
            src_ref=stat_out,
            dst_ref=stat_in.at[dst_slot],
            send_sem=stat_send.at[dst_slot],
            recv_sem=stat_recv.at[dst_slot],
            device_id=(t_rows[row], h_cols[col]),
            device_id_type=MESH,
        )

    def stat_arrived(slot):
        @pl.when(exists(slot))
        def _():
            pltpu.make_async_remote_copy(
                src_ref=stat_in.at[slot], dst_ref=stat_in.at[slot],
                send_sem=stat_send.at[slot], recv_sem=stat_recv.at[slot],
                device_id=(t_rows[1], h), device_id_type=MESH,
            ).wait_recv()

    for slot in (PP, L, R, OO, PL_, PR, OL, OR):
        @pl.when(exists(slot))
        def _():
            stat_travel(slot).start()

    for arr in (AQ, AG):
        pass_right((arr, 0))
        pass_left(False, (arr, 0))
    for chunk in range(chunks):
        pass_other(AG, chunk)
    pass_left(True, (AQ, 0))

    @pl.loop(0, heads)
    def _(hd):
        d = delta[hd]
        d = jnp.concatenate([d, d], axis=1)
        best = top[hd]

        acc = None
        for group, slots in enumerate(GROUPS):
            sides = [
                probs[slot, hd] * (dprobs[slot, hd] - d).astype(BF16) for slot in slots
            ]
            part = nn(
                jnp.concatenate(sides, axis=1),
                jnp.concatenate([tiles[AK, slot, hd] for slot in slots], axis=0),
            ) * jnp.exp2((group_max[group, hd] - best) * c2)
            acc = part if acc is None else acc + part
        staged[1, hd] = (acc * (scale / total[hd])).astype(BF16)

    store_all(1)

    place = lax.broadcasted_iota(jnp.int32, (rows, HEAD_DIM), 0)
    frame = (place >= 2 * cells).astype(jnp.int32)
    column = place - cells * (
        (place >= cells).astype(jnp.int32) + frame + (place >= 3 * cells).astype(jnp.int32)
    )
    own_0, own_1 = frame_len(TILE_SIDE * t), frame_len(TILE_SIDE * t + 1)
    live = column < jnp.where(frame == 1, own_1, own_0)

    def finish_out(hd):
        whole = jnp.concatenate(convolve(AV, hd, False), axis=0)
        staged[0, hd] = (attn[hd] / total[hd] + whole).astype(BF16)

    def finish_grads(hd):
        whole = jnp.concatenate(convolve(AG, hd, True), axis=0)
        staged[2, hd] = jnp.where(live, key_acc[hd] * scale, 0.0).astype(BF16)
        staged[3, hd] = (jnp.where(live, value_acc[hd], 0.0) + whole).astype(BF16)

    pass_left(True, (AG, 0))
    pass_right((AQ, 1))
    pass_left(False, (AQ, 1))
    for slot in (PP, OO):
        stat_arrived(slot)
    arrived_all((AQ, AG), (PP,), 0)
    arrived_all((AQ,), (OO,), 0)
    key_group(KEY_GROUPS[0], 0, finish_out)
    pass_left(True, (AQ, 1))
    pass_right((AG, 1))
    pass_left(False, (AG, 1))
    arrived_all((AQ, AG), (PP,), 1)
    arrived_all((AQ,), (OO,), 1)
    key_group(KEY_GROUPS[0], 1, finish_out)
    store_all(0)
    pass_left(True, (AG, 1))
    for group, beside in ((1, None), (2, finish_grads)):
        slots = KEY_GROUPS[group]
        for slot in slots:
            stat_arrived(slot)
        for chunk in range(chunks):
            arrived_all((AQ, AG), slots[1:], chunk)
            key_group(slots, chunk, beside)
    store_all(2)
    store_all(3)
    for arr, src_slot, to, chunk, also in sent:
        @pl.when(exists(src_slot, to, also=also))
        def _():
            travel(arr, src_slot, to, chunk).wait_send()

    for slot in range(1, 9):
        @pl.when(exists(slot))
        def _():
            stat_travel(slot).wait_send()

    for which in range(4):
        for hd in range(heads):
            store(which, hd).wait()


def hand_over(*refs):
    ins, outs, (held, in_sem, out_sem) = refs[:4], refs[4:8], refs[8:]
    arrive = [pltpu.make_async_copy(ins[i], held.at[i], in_sem.at[i]) for i in range(4)]
    leave = [pltpu.make_async_copy(held.at[i], outs[i], out_sem.at[i]) for i in range(4)]
    for copy in arrive:
        copy.start()
    for first, then in zip(arrive, leave, strict=True):
        first.wait()
        then.start()
    for copy in leave:
        copy.wait()


def shards(query_states, key_states, value_states, conv_weight, out_grad, tile_mask, clip_lengths):
    side_t, side_h, cells, channels = query_states.shape
    rows = side_t * side_h * cells
    padded = -(-rows // 128) * 128
    heads = channels // HEAD_DIM
    chunks = 2
    n_t, n_h = lax.axis_size("ta"), lax.axis_size("ha")
    flat = (rows, channels)
    any_space = pl.BlockSpec(memory_space=pl.ANY)
    outs = pl.pallas_call(
        functools.partial(kernel, heads, cells, rows, padded, n_t, n_h, chunks),
        out_shape=[jax.ShapeDtypeStruct(flat, BF16)] * 4,
        in_specs=[any_space] * 7,
        out_specs=[any_space] * 4,
        scratch_shapes=[
            pltpu.VMEM((4, 9, heads, padded, HEAD_DIM), BF16),
            pltpu.VMEM((9, heads, rows, padded), BF16),
            pltpu.VMEM((9, heads, rows, padded), F32),
            pltpu.VMEM((len(GROUPS), heads, rows, HEAD_DIM), F32),
            pltpu.VMEM((heads, rows, HEAD_DIM), F32),
            pltpu.VMEM((heads, rows, HEAD_DIM), F32),
            pltpu.VMEM((heads, rows, HEAD_DIM), F32),
            pltpu.VMEM((heads, rows, HEAD_DIM), F32),
            pltpu.VMEM((heads, rows, HEAD_DIM), F32),
            pltpu.VMEM((heads, rows, HEAD_DIM), F32),
            pltpu.VMEM((4, heads, rows, HEAD_DIM), BF16),
            pltpu.VMEM((9, 1, padded), F32),
            pltpu.VMEM((9, 1, padded), F32),
            pltpu.VMEM((padded, HEAD_DIM), F32),
            pltpu.VMEM((2 * heads, 1, padded), F32),
            pltpu.VMEM((9, 2 * heads, 1, padded), F32),
            pltpu.VMEM(conv_weight.shape, BF16),
            pltpu.VMEM((heads, conv_weight.shape[0], HEAD_DIM), F32),
            pltpu.VMEM((9, n_t, n_h), jnp.int32),
            pltpu.SMEM(clip_lengths.shape, jnp.int32),
            pltpu.SemaphoreType.DMA((4, heads)),
            pltpu.SemaphoreType.DMA((3,)),
            pltpu.SemaphoreType.DMA((4, heads)),
            pltpu.SemaphoreType.DMA((4, 9, chunks)),
            pltpu.SemaphoreType.DMA((4, 9, chunks)),
            pltpu.SemaphoreType.DMA((9,)),
            pltpu.SemaphoreType.DMA((9,)),
        ],
        compiler_params=pltpu.CompilerParams(
            collective_id=0, has_side_effects=True, vmem_limit_bytes=60 * 1024 * 1024
        ),
    )(
        query_states.reshape(flat),
        key_states.reshape(flat),
        value_states.reshape(flat),
        conv_weight,
        out_grad.reshape(flat),
        tile_mask.transpose(2, 0, 1),
        clip_lengths,
    )
    outs = pl.pallas_call(
        hand_over,
        out_shape=[jax.ShapeDtypeStruct(flat, BF16)] * 4,
        in_specs=[any_space] * 4,
        out_specs=[any_space] * 4,
        scratch_shapes=[
            pltpu.VMEM((4,) + flat, BF16),
            pltpu.SemaphoreType.DMA((4,)),
            pltpu.SemaphoreType.DMA((4,)),
        ],
    )(*outs)
    return tuple(out.reshape(query_states.shape) for out in outs)


def solution(mesh):
    tiled = P("ta", "ha", None, None)
    return jax.shard_map(
        shards,
        mesh=mesh,
        in_specs=(tiled, tiled, tiled, P(), tiled, P(), P()),
        out_specs=(tiled,) * 4,
        check_vma=False,
    )
```

```python
import functools
import math

import jax
import jax.numpy as jnp
from jax import lax
from jax.experimental import pallas as pl
from jax.experimental.pallas import tpu as pltpu
from jax.sharding import PartitionSpec as P

MESH = pl.DeviceIdType.MESH
HEAD_DIM = 128
TILE_SIDE = 2
F32 = jnp.float32
BF16 = jnp.bfloat16
BIG = 1e30
LOG2E = math.log2(math.e)

AK, AV, AQ, AG = 0, 1, 2, 3
OWN, L, R, PP, PL_, PR, OO, OL, OR = range(9)
GROUPS = ((OWN, PP), (OO,), (R, PR, OR), (L, PL_, OL))
KEY_GROUPS = ((OWN, PP, OO), (R, PR, OR), (L, PL_, OL))
Y_FIRST = ((AV, 1), (AG, 1))
FWD_UNROLL = 3
KEY_UNROLL = 3
Z_CHIPS = 12

LAST = (((1,), (1,)), ((), ()))


def nt(a, b):
    return lax.dot_general(a, b, LAST, preferred_element_type=F32)


def nn(a, b):
    return jnp.dot(a, b, preferred_element_type=F32)


def kernel(
    heads, cells, rows, padded, n_t, n_h, chunks,
    q_hbm, k_hbm, v_hbm, w_hbm, g_hbm, mask_hbm, clip_hbm,
    out_hbm, dq_hbm, dk_hbm, dv_hbm,
    tiles, probs, dprobs, group_max, top, total, attn, delta, key_acc, value_acc, staged,
    bias, penalty, stat_mat, stat_out, stat_in, w_ref, wf_ref, mask_ref, clip_ref,
    late_sem, load_sem, aux_sem, store_sem, send_sem, recv_sem, stat_send, stat_recv,
):
    scale = HEAD_DIM ** -0.5
    c2 = scale * LOG2E
    t = lax.axis_index("ta")
    h = lax.axis_index("ha")
    parity = lax.rem(t, 2)
    a_p = 1 - 2 * parity
    a_rows = (0, a_p, -a_p)
    b_cols = (0, -1, 1)
    t_rows = tuple(lax.rem(t + a + n_t, n_t) for a in a_rows)
    h_cols = tuple(lax.rem(h + b + n_h, n_h) for b in b_cols)
    flip = (0, 2, 1)
    hpc = heads // chunks
    has_row = (None, None, (t - a_p >= 0) & (t - a_p < n_t))
    has_col = (None, h > 0, h < n_h - 1)

    late_left = (h > 0) & (lax.rem(h, Z_CHIPS) == 0)
    to_early = (h < n_h - 1) & (lax.rem(h, Z_CHIPS) == Z_CHIPS - 1)

    def exists(*slots, also=None):
        found = jnp.bool_(True) if also is None else also
        for slot in slots:
            for there in (has_row[slot // 3], has_col[slot % 3]):
                if there is not None:
                    found = found & there
        return found

    def load(arr, hd):
        src = (k_hbm, v_hbm, q_hbm, g_hbm)[arr]
        return pltpu.make_async_copy(
            src.at[:, pl.ds(hd * HEAD_DIM, HEAD_DIM)],
            tiles.at[arr, OWN, hd, pl.ds(0, rows)],
            load_sem.at[arr, hd],
        )

    for chunk in range(chunks):
        for arr in (AK, AV):
            for hd in range(chunk * hpc, (chunk + 1) * hpc):
                load(arr, hd).start()
    for arr in (AQ, AG):
        for hd in range(heads):
            load(arr, hd).start()
    aux = (
        pltpu.make_async_copy(mask_hbm, mask_ref, aux_sem.at[0]),
        pltpu.make_async_copy(clip_hbm, clip_ref, aux_sem.at[1]),
        pltpu.make_async_copy(w_hbm, w_ref, aux_sem.at[2]),
    )
    for copy in aux:
        copy.start()

    barrier = pltpu.get_barrier_semaphore()
    for slot in range(1, 9):
        @pl.when(exists(slot, also=jnp.logical_not(to_early) if slot % 3 == R else None))
        def _():
            pl.semaphore_signal(
                barrier, inc=1, device_id=(t_rows[slot // 3], h_cols[slot % 3]), device_id_type=MESH
            )
    near_t = 2 + has_row[2].astype(jnp.int32)
    here_left = has_col[1] & jnp.logical_not(late_left)
    near_h = 1 + here_left.astype(jnp.int32) + has_col[2].astype(jnp.int32)
    pl.semaphore_wait(barrier, near_t * near_h - 1)
    for slot in (R, PR, OR):
        @pl.when(exists(slot, also=to_early))
        def _():
            pl.semaphore_signal(
                late_sem, inc=1, device_id=(t_rows[slot // 3], h_cols[slot % 3]), device_id_type=MESH
            )

    def travel(arr, src_slot, to, chunk):
        row, col = src_slot // 3, src_slot % 3
        if to in (L, R):
            dst_slot = 3 * row + flip[to]
            device = (t, h_cols[to])
        else:
            dst_slot = to + col
            device = (t_rows[to // 3], h)
        part = (pl.ds(chunk * hpc, hpc), pl.ds(0, rows))
        return pltpu.make_async_remote_copy(
            src_ref=tiles.at[(arr, src_slot) + part],
            dst_ref=tiles.at[(arr, dst_slot) + part],
            send_sem=send_sem.at[arr, {(OO, L): 9, (OO, R): 0}.get((src_slot, to), dst_slot), chunk],
            recv_sem=recv_sem.at[arr, dst_slot, chunk],
            device_id=device,
            device_id_type=MESH,
        )

    sent = []

    def send(arr, src_slot, targets):
        for chunk in range(chunks):
            send_chunk(arr, src_slot, targets, chunk)

    def send_chunk(arr, src_slot, targets, chunk, also=None):
        for to in targets:
            sent.append((arr, src_slot, to, chunk, also))

            @pl.when(exists(src_slot, to, also=also))
            def _():
                travel(arr, src_slot, to, chunk).start()

    def arrived_chunk(arr, slot, chunk):
        part = (pl.ds(chunk * hpc, hpc), pl.ds(0, rows))
        place = tiles.at[(arr, slot) + part]

        @pl.when(exists(slot))
        def _():
            pltpu.make_async_remote_copy(
                src_ref=place, dst_ref=place,
                send_sem=send_sem.at[arr, slot, chunk], recv_sem=recv_sem.at[arr, slot, chunk],
                device_id=(t_rows[1], h), device_id_type=MESH,
            ).wait_recv()

    def arrived(arr, slot):
        for chunk in range(chunks):
            arrived_chunk(arr, slot, chunk)

    for chunk in range(chunks):
        for arr in (AK, AV):
            for hd in range(chunk * hpc, (chunk + 1) * hpc):
                load(arr, hd).wait()
            send_chunk(arr, OWN, (OO, R, PP), chunk)
            send_chunk(arr, OWN, (L,), chunk, jnp.logical_not(late_left))
    for arr in (AQ, AG):
        for hd in range(heads):
            load(arr, hd).wait()
        send(arr, OWN, (PP,))

    def pass_side(arr, side, chunk):
        arrived_chunk(arr, side, chunk)
        send_chunk(arr, side, (PP,), chunk)
        if (arr, chunk) not in Y_FIRST:
            send_chunk(arr, side, (OO,), chunk)

    def pass_right(*parts):
        for arr, chunk in parts:
            pass_side(arr, R, chunk)

    def pass_left(*parts):
        for arr, chunk in parts:
            pass_side(arr, L, chunk)

    def pass_other(arr, chunk):
        arrived_chunk(arr, OO, chunk)
        if (arr, chunk) in Y_FIRST:
            send_chunk(arr, OO, (L,), chunk)
            send_chunk(arr, OO, (R,), chunk)

    @pl.loop(0, 4 * 9)
    def _(i):
        tiles[i // 9, i % 9, :, pl.ds(rows, padded - rows), :] = jnp.zeros(
            (heads, padded - rows, HEAD_DIM), BF16
        )

    for slot in range(1, 9):
        if slot != PP:
            @pl.when(jnp.logical_not(exists(slot)))
            def _():
                stat_in[slot] = jnp.zeros(stat_in.shape[1:], F32)

                @pl.loop(0, 4 * heads)
                def _(i):
                    tiles[i // heads, slot, i % heads, pl.ds(0, rows), :] = jnp.zeros(
                        (rows, HEAD_DIM), BF16
                    )

    for copy in aux:
        copy.wait()

    lane = lax.broadcasted_iota(jnp.int32, (1, padded), 1)
    tile_frame = (lane >= 2 * cells).astype(jnp.int32)
    column = lane - cells * (
        (lane >= cells).astype(jnp.int32) + tile_frame + (lane >= 3 * cells).astype(jnp.int32)
    )
    shape = mask_ref.shape[1:]
    it = lax.broadcasted_iota(jnp.int32, shape, 0)
    ih = lax.broadcasted_iota(jnp.int32, shape, 1)

    def frame_len(frame):
        live = clip_ref[jnp.clip(frame, 0, TILE_SIDE * n_t - 1)]
        return jnp.where((frame >= 0) & (frame < TILE_SIDE * n_t), live, 0)

    def entry(index, at_t, at_h):
        here = (it == at_t) & (ih == at_h)
        picked = jnp.where(here, mask_ref[index], 0).astype(F32)
        return jnp.sum(picked, axis=(0, 1), keepdims=True)

    for slot in range(9):
        a, b = a_rows[slot // 3], b_cols[slot % 3]
        index = 3 * (a + 1) + (b + 1)
        first = TILE_SIDE * (t + a)
        len_0, len_1 = frame_len(first), frame_len(first + 1)
        inside = ((h + b >= 0) & (h + b < n_h)).astype(jnp.int32)
        live = jnp.where(tile_frame == 1, len_1 * inside, len_0 * inside)
        seen = (column < live) & (lane < rows)
        keep = jnp.where(seen, entry(index, t, h), 0.0)
        bias[slot] = jnp.where(keep > 0.5, 0.0, -BIG)
        facing = entry(8 - index, t + a, h + b)
        penalty[slot] = jnp.where((lane < rows), jnp.where(facing > 0.5, 0.0, BIG), BIG)

    def forward_group(group, chunk):
        slots = GROUPS[group]

        @pl.loop(chunk * hpc, (chunk + 1) * hpc, unroll=FWD_UNROLL)
        def _(hd):
            q = tiles[AQ, OWN, hd, pl.ds(0, rows), :]
            g = tiles[AG, OWN, hd, pl.ds(0, rows), :]
            scores = [nt(q, tiles[AK, slot, hd]) + bias[slot] for slot in slots]
            m = jnp.max(functools.reduce(jnp.maximum, scores), axis=-1, keepdims=True)
            ps = [jnp.exp2((s - m) * c2) for s in scores]
            row_sum = jnp.sum(functools.reduce(jnp.add, ps), axis=-1, keepdims=True)
            ps = [p.astype(BF16) for p in ps]
            for slot, p in zip(slots, ps, strict=True):
                probs[slot, hd] = p
                dprobs[slot, hd] = nt(g, tiles[AV, slot, hd])
            part = nn(
                jnp.concatenate(ps, axis=1),
                jnp.concatenate([tiles[AV, slot, hd] for slot in slots], axis=0),
            )
            m = jnp.broadcast_to(m, (rows, HEAD_DIM))
            group_max[group, hd] = m
            if group == 0:
                top[hd] = m
                total[hd] = jnp.broadcast_to(row_sum, (rows, HEAD_DIM))
                attn[hd] = part
            else:
                old = top[hd]
                new = jnp.maximum(old, m)
                keep_old = jnp.exp2((old - new) * c2)
                keep_new = jnp.exp2((m - new) * c2)
                top[hd] = new
                total[hd] = total[hd] * keep_old + row_sum * keep_new
                attn[hd] = attn[hd] * keep_old + part * keep_new

    def key_group(slots, chunk, beside=None):
        @pl.loop(chunk * hpc, (chunk + 1) * hpc, unroll=KEY_UNROLL)
        def _(hd):
            k = tiles[AK, OWN, hd, pl.ds(0, rows), :]
            v = tiles[AV, OWN, hd, pl.ds(0, rows), :]
            ps, dss = [], []
            for slot in slots:
                log_total = stat_in[slot, 2 * hd] + penalty[slot]
                p = jnp.exp2(nt(k, tiles[AQ, slot, hd]) * c2 - log_total)
                ps.append(p.astype(BF16))
                ds = p * (nt(v, tiles[AG, slot, hd]) - stat_in[slot, 2 * hd + 1])
                dss.append(ds.astype(BF16))
            for acc, sides, arr in ((value_acc, ps, AG), (key_acc, dss, AQ)):
                part = nn(
                    jnp.concatenate(sides, axis=1),
                    jnp.concatenate([tiles[arr, slot, hd] for slot in slots], axis=0),
                )
                if slots[0] == OWN:
                    acc[hd] = part
                else:
                    acc[hd] += part
            if beside is not None:
                beside(hd)

    def convolve(arr, hd, flipped):
        r_minus, r_plus = 2 - parity, 1 + parity
        in_t = ((t > 0).astype(F32), None, None, (t < n_t - 1).astype(F32))
        in_h = ((h > 0).astype(F32), None, None, (h < n_h - 1).astype(F32))
        source = {}
        for big_i in range(4):
            row = (r_minus, 0, 0, r_plus)[big_i]
            for big_j in range(4):
                col = (1, 0, 0, 2)[big_j]
                i, j = (1, 0, 1, 0)[big_i], (1, 0, 1, 0)[big_j]
                whole = tiles[arr, 3 * row + col, hd, pl.ds(0, rows), :].astype(F32)
                start = (2 * i + j) * cells
                piece = whole[start:start + cells]
                for factor in (in_t[big_i], in_h[big_j]):
                    if factor is not None:
                        piece = piece * factor
                source[big_i, big_j] = piece
        place = lax.broadcasted_iota(jnp.int32, (cells, HEAD_DIM), 0)
        pieces = []
        for i in range(2):
            for j in range(2):
                sums = []
                for dw in range(3):
                    acc = None
                    for dt in range(3):
                        for dh in range(3):
                            o = 9 * dt + 3 * dh + dw
                            o = 26 - o if flipped else o
                            term = source[i + dt, j + dh] * wf_ref[hd, pl.ds(o, 1), :]
                            acc = term if acc is None else acc + term
                    sums.append(acc)
                before = jnp.where(place == 0, 0.0, pltpu.roll(sums[0], 1, 0))
                after = jnp.where(place == cells - 1, 0.0, pltpu.roll(sums[2], cells - 1, 0))
                pieces.append(sums[1] + before + after)
        return pieces

    def store(which, hd):
        dst = (out_hbm, dq_hbm, dk_hbm, dv_hbm)[which]
        return pltpu.make_async_copy(
            staged.at[which, hd],
            dst.at[:, pl.ds(hd * HEAD_DIM, HEAD_DIM)],
            store_sem.at[which, hd],
        )

    def store_all(which):
        for hd in range(heads):
            store(which, hd).start()

    for hd in range(heads):
        wf_ref[hd] = w_ref[:, hd * HEAD_DIM:(hd + 1) * HEAD_DIM].astype(F32)

    arrived(AK, PP)
    arrived(AV, PP)
    for chunk in range(chunks):
        forward_group(0, chunk)
    first, second = ((AK, 0), (AV, 0)), ((AK, 1), (AV, 1))
    pass_right(*first)
    @pl.when(late_left)
    def _():
        pl.semaphore_wait(late_sem, near_t)

    for arr, chunk in first + second:
        send_chunk(arr, OWN, (L,), chunk, late_left)
    pass_left(*first)
    for arr, chunk in first:
        pass_other(arr, chunk)
    forward_group(1, 0)

    for arr, chunk in second:
        pass_other(arr, chunk)
    for chunk in range(chunks):
        for arr in (AQ, AG):
            send_chunk(arr, OWN, (L, R), chunk)
    forward_group(1, 1)

    def arrived_all(arrs, slots, chunk):
        for slot in slots:
            for arr in arrs:
                arrived_chunk(arr, slot, chunk)

    arrived_all((AK, AV), (PR, OR), 0)
    forward_group(2, 0)
    pass_right(*second)
    pass_left(*second)
    for chunk in range(chunks):
        for arr in (AQ, AG):
            send_chunk(arr, OWN, (OO,), chunk)
    arrived_all((AK, AV), (PR, OR), 1)
    forward_group(2, 1)
    arrived_all((AK, AV), (PL_, OL), 0)
    forward_group(3, 0)
    arrived_all((AK, AV), (PL_, OL), 1)
    forward_group(3, 1)

    stat_mat[...] = jnp.zeros_like(stat_mat)

    @pl.loop(0, heads)
    def _(hd):
        g = tiles[AG, OWN, hd, pl.ds(0, rows), :].astype(F32)
        sums = total[hd]
        inverse = 1.0 / sums
        d = jnp.sum(g * attn[hd], axis=-1, keepdims=True) * inverse
        delta[hd] = d
        log_total = top[hd] * c2 + jnp.log(sums) * LOG2E
        lanes = lax.broadcasted_iota(jnp.int32, (rows, HEAD_DIM), 1)
        stat_mat[pl.ds(0, rows), :] = jnp.where(
            lanes == 2 * hd, log_total, jnp.where(lanes == 2 * hd + 1, d, stat_mat[pl.ds(0, rows), :])
        )

    as_rows = stat_mat[...].T
    for i in range(2 * heads):
        stat_out[i] = as_rows[i:i + 1]
        stat_in[OWN, i] = as_rows[i:i + 1]

    def stat_travel(slot):
        row, col = slot // 3, slot % 3
        dst_slot = 3 * row + flip[col]
        return pltpu.make_async_remote_copy(
            src_ref=stat_out,
            dst_ref=stat_in.at[dst_slot],
            send_sem=stat_send.at[dst_slot],
            recv_sem=stat_recv.at[dst_slot],
            device_id=(t_rows[row], h_cols[col]),
            device_id_type=MESH,
        )

    def stat_arrived(slot):
        @pl.when(exists(slot))
        def _():
            pltpu.make_async_remote_copy(
                src_ref=stat_in.at[slot], dst_ref=stat_in.at[slot],
                send_sem=stat_send.at[slot], recv_sem=stat_recv.at[slot],
                device_id=(t_rows[1], h), device_id_type=MESH,
            ).wait_recv()

    for slot in (PP, L, R, OO, PL_, PR, OL, OR):
        @pl.when(exists(slot))
        def _():
            stat_travel(slot).start()

    for arr in (AQ, AG):
        pass_right((arr, 0))
        pass_left((arr, 0))
    for chunk in range(chunks):
        pass_other(AG, chunk)

    @pl.loop(0, heads)
    def _(hd):
        d = delta[hd]
        d = jnp.concatenate([d, d], axis=1)
        best = top[hd]

        acc = None
        for group, slots in enumerate(GROUPS):
            sides = [
                probs[slot, hd] * (dprobs[slot, hd] - d).astype(BF16) for slot in slots
            ]
            part = nn(
                jnp.concatenate(sides, axis=1),
                jnp.concatenate([tiles[AK, slot, hd] for slot in slots], axis=0),
            ) * jnp.exp2((group_max[group, hd] - best) * c2)
            acc = part if acc is None else acc + part
        staged[1, hd] = (acc * (scale / total[hd])).astype(BF16)

    store_all(1)

    place = lax.broadcasted_iota(jnp.int32, (rows, HEAD_DIM), 0)
    frame = (place >= 2 * cells).astype(jnp.int32)
    column = place - cells * (
        (place >= cells).astype(jnp.int32) + frame + (place >= 3 * cells).astype(jnp.int32)
    )
    own_0, own_1 = frame_len(TILE_SIDE * t), frame_len(TILE_SIDE * t + 1)
    live = column < jnp.where(frame == 1, own_1, own_0)

    def finish_out(hd):
        whole = jnp.concatenate(convolve(AV, hd, False), axis=0)
        staged[0, hd] = (attn[hd] / total[hd] + whole).astype(BF16)

    def finish_grads(hd):
        whole = jnp.concatenate(convolve(AG, hd, True), axis=0)
        staged[2, hd] = jnp.where(live, key_acc[hd] * scale, 0.0).astype(BF16)
        staged[3, hd] = (jnp.where(live, value_acc[hd], 0.0) + whole).astype(BF16)

    pass_right((AQ, 1))
    pass_left((AQ, 1))
    for slot in (PP, OO):
        stat_arrived(slot)
    arrived_all((AQ, AG), (PP,), 0)
    arrived_all((AQ,), (OO,), 0)
    key_group(KEY_GROUPS[0], 0, finish_out)
    pass_right((AG, 1))
    pass_left((AG, 1))
    arrived_all((AQ, AG), (PP,), 1)
    arrived_all((AQ,), (OO,), 1)
    key_group(KEY_GROUPS[0], 1, finish_out)
    store_all(0)
    for group, beside in ((1, None), (2, finish_grads)):
        slots = KEY_GROUPS[group]
        for slot in slots:
            stat_arrived(slot)
        for chunk in range(chunks):
            arrived_all((AQ, AG), slots[1:], chunk)
            key_group(slots, chunk, beside)
    store_all(2)
    store_all(3)
    for arr, src_slot, to, chunk, also in sent:
        @pl.when(exists(src_slot, to, also=also))
        def _():
            travel(arr, src_slot, to, chunk).wait_send()

    for slot in range(1, 9):
        @pl.when(exists(slot))
        def _():
            stat_travel(slot).wait_send()

    for which in range(4):
        for hd in range(heads):
            store(which, hd).wait()


def hand_over(*refs):
    ins, outs, (held, in_sem, out_sem) = refs[:4], refs[4:8], refs[8:]
    arrive = [pltpu.make_async_copy(ins[i], held.at[i], in_sem.at[i]) for i in range(4)]
    leave = [pltpu.make_async_copy(held.at[i], outs[i], out_sem.at[i]) for i in range(4)]
    for copy in arrive:
        copy.start()
    for first, then in zip(arrive, leave, strict=True):
        first.wait()
        then.start()
    for copy in leave:
        copy.wait()


def shards(query_states, key_states, value_states, conv_weight, out_grad, tile_mask, clip_lengths):
    side_t, side_h, cells, channels = query_states.shape
    rows = side_t * side_h * cells
    padded = -(-rows // 128) * 128
    heads = channels // HEAD_DIM
    chunks = 2
    n_t, n_h = lax.axis_size("ta"), lax.axis_size("ha")
    flat = (rows, channels)
    any_space = pl.BlockSpec(memory_space=pl.ANY)
    outs = pl.pallas_call(
        functools.partial(kernel, heads, cells, rows, padded, n_t, n_h, chunks),
        out_shape=[jax.ShapeDtypeStruct(flat, BF16)] * 4,
        in_specs=[any_space] * 7,
        out_specs=[any_space] * 4,
        scratch_shapes=[
            pltpu.VMEM((4, 9, heads, padded, HEAD_DIM), BF16),
            pltpu.VMEM((9, heads, rows, padded), BF16),
            pltpu.VMEM((9, heads, rows, padded), F32),
            pltpu.VMEM((len(GROUPS), heads, rows, HEAD_DIM), F32),
            pltpu.VMEM((heads, rows, HEAD_DIM), F32),
            pltpu.VMEM((heads, rows, HEAD_DIM), F32),
            pltpu.VMEM((heads, rows, HEAD_DIM), F32),
            pltpu.VMEM((heads, rows, HEAD_DIM), F32),
            pltpu.VMEM((heads, rows, HEAD_DIM), F32),
            pltpu.VMEM((heads, rows, HEAD_DIM), F32),
            pltpu.VMEM((4, heads, rows, HEAD_DIM), BF16),
            pltpu.VMEM((9, 1, padded), F32),
            pltpu.VMEM((9, 1, padded), F32),
            pltpu.VMEM((padded, HEAD_DIM), F32),
            pltpu.VMEM((2 * heads, 1, padded), F32),
            pltpu.VMEM((9, 2 * heads, 1, padded), F32),
            pltpu.VMEM(conv_weight.shape, BF16),
            pltpu.VMEM((heads, conv_weight.shape[0], HEAD_DIM), F32),
            pltpu.VMEM((9, n_t, n_h), jnp.int32),
            pltpu.SMEM(clip_lengths.shape, jnp.int32),
            pltpu.SemaphoreType.REGULAR,
            pltpu.SemaphoreType.DMA((4, heads)),
            pltpu.SemaphoreType.DMA((3,)),
            pltpu.SemaphoreType.DMA((4, heads)),
            pltpu.SemaphoreType.DMA((4, 10, chunks)),
            pltpu.SemaphoreType.DMA((4, 9, chunks)),
            pltpu.SemaphoreType.DMA((9,)),
            pltpu.SemaphoreType.DMA((9,)),
        ],
        compiler_params=pltpu.CompilerParams(
            collective_id=0, has_side_effects=True, vmem_limit_bytes=60 * 1024 * 1024
        ),
    )(
        query_states.reshape(flat),
        key_states.reshape(flat),
        value_states.reshape(flat),
        conv_weight,
        out_grad.reshape(flat),
        tile_mask.transpose(2, 0, 1),
        clip_lengths,
    )
    outs = pl.pallas_call(
        hand_over,
        out_shape=[jax.ShapeDtypeStruct(flat, BF16)] * 4,
        in_specs=[any_space] * 4,
        out_specs=[any_space] * 4,
        scratch_shapes=[
            pltpu.VMEM((4,) + flat, BF16),
            pltpu.SemaphoreType.DMA((4,)),
            pltpu.SemaphoreType.DMA((4,)),
        ],
    )(*outs)
    return tuple(out.reshape(query_states.shape) for out in outs)


def solution(mesh):
    tiled = P("ta", "ha", None, None)
    return jax.shard_map(
        shards,
        mesh=mesh,
        in_specs=(tiled, tiled, tiled, P(), tiled, P(), P()),
        out_specs=(tiled,) * 4,
        check_vma=False,
    )
```
